512 devices in a mesh: row: 32 (over x, z), orb: 16 (over y, core).
Axes of the slice: x: 4, y: 8, z: 8, core: 2. Of those that a mesh axis runs over, the one named last changes fastest.
Arguments:
- orbitals: float32 [4096, 4096], P('row', 'orb'), may hold values from -700 to 700
Outputs:
- updated: float32 [4096, 4096], P('row', 'orb')
The draws below stay inside these ranges and needn't reach their ends.
All inputs are finite; a program needn't handle non-finite values.
Results may differ from the reference program's by a relative error of at most 0.0065.
Values sent between devices are 32-bit elements; how exact they have to be, the bound alone decides.
No kernel may reach another device: no remote copies, remote signals or barrier semaphores. Data moves between devices by JAX's collectives and lax.ppermute only.
A program may use at most 64 MiB of HBM per device.

```python
import math
import jax
import jax.numpy as jnp
from jax import lax

BLK = 256
TICKS = 2
NR = 4096
NORB = 4096


def draw_orbitals(key, part):
    keys = jax.random.split(jax.random.fold_in(key, 11), 5)
    ramp = 1.0 + 2.0 * jnp.arange(NR, dtype=jnp.float32) / NR
    noise = jax.random.truncated_normal(keys[0], -5.0, 5.0, (NR, NORB), jnp.float32)
    rowfac = jnp.exp(jax.random.uniform(keys[1], (NR, 1), jnp.float32, math.log(0.7), math.log(1.4)))
    strength = 0.5
    left = jax.random.uniform(keys[2], (NR, 8), jnp.float32, -1.7, 1.7)
    right = jax.random.uniform(keys[3], (8, NORB), jnp.float32, -1.7, 1.7)
    shared = jnp.dot(left, right) * (strength / math.sqrt(8.0))
    colfac = jnp.exp(jax.random.uniform(keys[4], (1, NORB), jnp.float32, math.log(0.5), math.log(2.0)))
    return (noise + shared) * rowfac * ramp[:, None] * colfac


def setup_inputs(seed: int = 0) -> dict:
    splits = jax.random.split(jax.random.key(seed), 2)
    return {
        "orbitals": draw_orbitals(jax.random.fold_in(splits[1], 71), 0),
    }


def finish(block):
    gram = jnp.dot(block.T, block, precision=lax.Precision.HIGHEST) / NR
    lower = jnp.linalg.cholesky(gram)
    ident = jnp.eye(block.shape[1], dtype=block.dtype)
    inverse = lax.linalg.triangular_solve(lower, ident, left_side=True, lower=True)
    return jnp.dot(block, inverse.T, precision=lax.Precision.HIGHEST)

def reference(orbitals):
    work = orbitals
    for tick in range(TICKS):
        start = tick * BLK
        finish_col = start + BLK
        basis = finish(work[:, start:finish_col])
        rest = work[:, finish_col:]
        coef = jnp.dot(basis.T, rest, precision=lax.Precision.HIGHEST) / NR
        rest = rest - jnp.dot(basis, coef, precision=lax.Precision.HIGHEST)
        work = jnp.concatenate([work[:, :start], basis, rest], axis=1)
    return work
```

```python
import jax
import jax.numpy as jnp
from jax import lax
from jax.experimental import pallas as pl
from jax.experimental.pallas import tpu as pltpu
from jax.sharding import PartitionSpec as P

SUB = 8
LANE = 128
EXACT = lax.Precision.HIGHEST


def dot(left, right, left_dim=1, right_dim=0):
    dims = (((left_dim,), (right_dim,)), ((), ()))
    return lax.dot_general(
        left, right, dims, precision=EXACT, preferred_element_type=jnp.float32
    )


def small_inverse(diag):
    rows = [list(line) for line in diag]
    low = [[None] * SUB for _ in range(SUB)]
    root = []
    for j in range(SUB):
        root.append(lax.rsqrt(rows[j][j]))
        for i in range(j + 1, SUB):
            low[i][j] = rows[i][j] * root[j]
        for i in range(j + 1, SUB):
            for k in range(j + 1, i + 1):
                rows[i][k] = rows[i][k] - low[i][j] * low[k][j]
    inv = [[None] * SUB for _ in range(SUB)]
    for j in range(SUB):
        inv[j][j] = root[j]
        for i in range(j + 1, SUB):
            total = low[i][j] * inv[j][j]
            for m in range(j + 1, i):
                total = total + low[i][m] * inv[m][j]
            inv[i][j] = -(root[i] * total)
    return inv


def factor(block):
    shape = (SUB, LANE)
    lane = lax.broadcasted_iota(jnp.int32, shape, 1)
    sub = lax.broadcasted_iota(jnp.int32, shape, 0)
    count = LANE // SUB
    tiles = [block[SUB * t : SUB * (t + 1), :] for t in range(count)]
    for k in range(count):
        base = SUB * k
        inside = (lane >= base) & (lane < base + SUB)
        own = tiles[k]
        cols = [jnp.broadcast_to(own[:, base + j : base + j + 1], shape) for j in range(SUB)]
        inv = small_inverse(
            [[jnp.broadcast_to(cols[j][i : i + 1, :], shape) for j in range(i + 1)] for i in range(SUB)]
        )
        cleared = jnp.where(inside, jnp.where(lane - base == sub, 1.0, 0.0), own)
        raw = [jnp.broadcast_to(cleared[i : i + 1, :], shape) for i in range(SUB)]
        done = []
        for i in range(SUB):
            total = inv[i][0] * raw[0]
            for m in range(1, i + 1):
                total = total + inv[i][m] * raw[m]
            done.append(total)
        for t in range(k + 1, count):
            col = [jnp.broadcast_to(tiles[t][:, base + j : base + j + 1], shape) for j in range(SUB)]
            rest = jnp.where(inside, 0.0, tiles[t])
            for j in range(SUB):
                left = inv[j][0] * col[0]
                for m in range(1, j + 1):
                    left = left + inv[j][m] * col[m]
                rest = rest - left * done[j]
            tiles[t] = rest
        row = done[0]
        for i in range(1, SUB):
            row = jnp.where(sub == i, done[i], row)
        tiles[k] = row
    return jnp.concatenate(tiles, axis=0)


def span(i):
    return slice(LANE * i, LANE * (i + 1))


HALVES = (((0, 0), (0, 1), None, (1, 1), (0, 2), (0, 3)), ((2, 2), (2, 3), None, (3, 3), (1, 2), (1, 3)))


def inverse_kernel(core_ref, mine_ref, other_ref, inv_ref, work_ref):
    n = inv_ref.shape[0]
    blocks = n // LANE
    first = core_ref[0] == 0
    work_ref[...] = jnp.zeros_like(work_ref)
    for half in range(2):
        for at, place in enumerate(HALVES[half]):
            if place is not None:
                mine, other = mine_ref[span(at), :], other_ref[span(at), :]
                tile = jnp.where(first == (half == 0), mine, other)
                work_ref[span(place[0]), span(place[1])] = tile
    for k in range(blocks):
        done = factor(work_ref[span(k), span(k)])
        row = lax.broadcasted_iota(jnp.int32, done.shape, 0)
        col = lax.broadcasted_iota(jnp.int32, done.shape, 1)
        done = jnp.where(row >= col, done, 0.0)
        work_ref[span(k), :] = dot(done, work_ref[span(k), :])
        work_ref[span(k), span(k)] = done
        for i in range(k + 1, blocks):
            up = work_ref[span(k), span(i)]
            work_ref[span(i), span(k)] = jnp.zeros((LANE, LANE), jnp.float32)
            work_ref[span(i), :] = work_ref[span(i), :] - dot(up, work_ref[span(k), :], 0, 0)
    for i in range(blocks):
        split = LANE * (i + 1)
        inv_ref[span(i), :split] = work_ref[span(i), :split]
        if split < n:
            inv_ref[span(i), split:] = jnp.zeros((LANE, n - split), jnp.float32)


def inverse_factor(core, mine, other, n):
    return pl.pallas_call(
        inverse_kernel,
        out_shape=jax.ShapeDtypeStruct((n, n), jnp.float32),
        in_specs=[pl.BlockSpec(memory_space=pltpu.SMEM)] + [pl.BlockSpec(memory_space=pltpu.VMEM)] * 2,
        out_specs=pl.BlockSpec(memory_space=pltpu.VMEM),
        scratch_shapes=[pltpu.VMEM((n, n), jnp.float32)],
        name="inverse_factor",
    )(core, mine, other)


def finish_kernel(index_ref, zero_ref, one_ref, inv_ref, gram_ref, own_ref, out_ref):
    width = own_ref.shape[1]
    index = index_ref[0]

    @pl.when(index == 0)
    def _():
        out_ref[...] = dot(zero_ref[...], inv_ref[:width, :width], 1, 1)

    @pl.when(index == 1)
    def _():
        out_ref[...] = dot(zero_ref[...], inv_ref[width:, :width], 1, 1) + dot(
            one_ref[...], inv_ref[width:, width:], 1, 1
        )

    @pl.when(index > 1)
    def _():
        top = dot(inv_ref[:width, :width], gram_ref[:width, :])
        low = dot(inv_ref[width:, :], gram_ref[...])
        basis = dot(zero_ref[...], inv_ref[:width, :width], 1, 1)
        later = dot(zero_ref[...], inv_ref[width:, :width], 1, 1) + dot(
            one_ref[...], inv_ref[width:, width:], 1, 1
        )
        out_ref[...] = own_ref[...] - dot(basis, top) - dot(later, low)


def finish(index, zero, one, inverse, gram, own):
    return pl.pallas_call(
        finish_kernel,
        out_shape=jax.ShapeDtypeStruct(own.shape, own.dtype),
        in_specs=[pl.BlockSpec(memory_space=pltpu.SMEM)] + [pl.BlockSpec(memory_space=pltpu.VMEM)] * 5,
        out_specs=pl.BlockSpec(memory_space=pltpu.VMEM),
        name="finish",
    )(index, zero, one, inverse, gram, own)


def swapped(pieces, axis):
    return lax.all_to_all(pieces, axis, 0, 0, tiled=True)


def spread(piece, axis):
    return swapped(jnp.broadcast_to(piece[None], (lax.axis_size(axis), *piece.shape)), axis)


def on_device(own):
    rows, width = own.shape
    many, groups = lax.axis_size("row"), lax.axis_size("orb")
    count = rows * many
    index = lax.axis_index("orb")
    core = index % 2
    pairs = [(i, i ^ 1) for i in range(groups)]

    share = swapped(own.reshape(groups, -1, width), "orb")[:2]
    pair = lax.ppermute(own, "orb", pairs)
    left = jnp.where(core == 0, own[:, :LANE], pair[:, LANE:])
    right = jnp.where(core == 0, pair, own)
    square = dot(own, own, 0, 0) / count
    cross = dot(left, right, 0, 0) / count
    tiles = [square[:LANE, :LANE], square[:LANE, LANE:], square[LANE:, :LANE], square[LANE:, LANE:]]
    tiles += [cross[:, :LANE], cross[:, LANE:]]
    half = jnp.concatenate(tiles, axis=0)
    half = jnp.sum(swapped(half.reshape(many, -1, LANE), "row"), axis=0)

    blocks = spread(share, "orb")
    zero, one = blocks[:, 0].reshape(rows, width), blocks[:, 1].reshape(rows, width)
    half = jnp.where(core == 0, *spread(half, "orb")[:2])
    mine = spread(half, "row").reshape(-1, LANE)
    other = lax.ppermute(mine, "orb", pairs)

    gram = jnp.concatenate([dot(zero, own, 0, 0), dot(one, own, 0, 0)], axis=0) / count
    gram = jnp.sum(swapped(gram.reshape(many, -1, width), "row"), axis=0)
    gram = spread(gram, "row").reshape(-1, width)

    inverse = inverse_factor(core.reshape(1), mine, other, 2 * width)
    return finish(index.reshape(1), zero, one, inverse, gram, own)


def solution(mesh):
    return jax.shard_map(
        on_device,
        mesh=mesh,
        in_specs=(P("row", "orb"),),
        out_specs=P("row", "orb"),
        check_vma=False,
    )
```

```python
import functools

import jax
import jax.numpy as jnp
from jax import lax
from jax.experimental import pallas as pl
from jax.experimental.pallas import tpu as pltpu
from jax.sharding import PartitionSpec as P

SUB = 8
LANE = 128
EXACT = lax.Precision.HIGHEST


def dot(left, right, left_dim=1, right_dim=0):
    dims = (((left_dim,), (right_dim,)), ((), ()))
    return lax.dot_general(
        left, right, dims, precision=EXACT, preferred_element_type=jnp.float32
    )


def small_inverse(diag):
    rows = [list(line) for line in diag]
    low = [[None] * SUB for _ in range(SUB)]
    root = []
    for j in range(SUB):
        root.append(lax.rsqrt(rows[j][j]))
        for i in range(j + 1, SUB):
            low[i][j] = rows[i][j] * root[j]
        for i in range(j + 1, SUB):
            for k in range(j + 1, i + 1):
                rows[i][k] = rows[i][k] - low[i][j] * low[k][j]
    inv = [[None] * SUB for _ in range(SUB)]
    for j in range(SUB):
        inv[j][j] = root[j]
        for i in range(j + 1, SUB):
            total = low[i][j] * inv[j][j]
            for m in range(j + 1, i):
                total = total + low[i][m] * inv[m][j]
            inv[i][j] = -(root[i] * total)
    return inv


def factor(block):
    shape = (SUB, LANE)
    lane = lax.broadcasted_iota(jnp.int32, shape, 1)
    sub = lax.broadcasted_iota(jnp.int32, shape, 0)
    count = LANE // SUB
    tiles = [block[SUB * t : SUB * (t + 1), :] for t in range(count)]
    for k in range(count):
        base = SUB * k
        inside = (lane >= base) & (lane < base + SUB)
        own = tiles[k]
        cols = [jnp.broadcast_to(own[:, base + j : base + j + 1], shape) for j in range(SUB)]
        inv = small_inverse(
            [[jnp.broadcast_to(cols[j][i : i + 1, :], shape) for j in range(i + 1)] for i in range(SUB)]
        )
        cleared = jnp.where(inside, jnp.where(lane - base == sub, 1.0, 0.0), own)
        raw = [jnp.broadcast_to(cleared[i : i + 1, :], shape) for i in range(SUB)]
        done = []
        for i in range(SUB):
            total = inv[i][0] * raw[0]
            for m in range(1, i + 1):
                total = total + inv[i][m] * raw[m]
            done.append(total)
        for t in range(k + 1, count):
            col = [jnp.broadcast_to(tiles[t][:, base + j : base + j + 1], shape) for j in range(SUB)]
            rest = jnp.where(inside, 0.0, tiles[t])
            for j in range(SUB):
                left = inv[j][0] * col[0]
                for m in range(1, j + 1):
                    left = left + inv[j][m] * col[m]
                rest = rest - left * done[j]
            tiles[t] = rest
        row = done[0]
        for i in range(1, SUB):
            row = jnp.where(sub == i, done[i], row)
        tiles[k] = row
    return jnp.concatenate(tiles, axis=0)


def span(i, size=LANE):
    return slice(size * i, size * (i + 1))


HALVES = (((0, 0), (0, 1), None, (1, 1), (0, 2), (0, 3)), ((2, 2), (2, 3), None, (3, 3), (1, 2), (1, 3)))
GRAM = 24
BASIS = 32


def call(kernel, outs, scalar, *args, scratch=(), name):
    return pl.pallas_call(
        kernel,
        out_shape=[jax.ShapeDtypeStruct(shape, jnp.float32) for shape in outs],
        in_specs=[pl.BlockSpec(memory_space=pltpu.SMEM)] + [pl.BlockSpec(memory_space=pltpu.VMEM)] * len(args),
        out_specs=[pl.BlockSpec(memory_space=pltpu.VMEM)] * len(outs),
        scratch_shapes=[pltpu.VMEM(shape, jnp.float32) for shape in scratch],
        name=name,
    )(scalar.reshape(1), *args)


def half_kernel(core_ref, own_ref, pair_ref, half_ref, *, count):
    own, pair = own_ref[...], pair_ref[...]
    first = core_ref[0] == 0
    left = jnp.where(first, own[:, :LANE], pair[:, LANE:])
    right = jnp.where(first, pair, own)
    square = dot(own, own, 0, 0) / count
    cross = dot(left, right, 0, 0) / count
    for i in range(4):
        half_ref[span(i), :] = square[span(i // 2), span(i % 2)]
    for i in range(2):
        half_ref[span(4 + i), :] = cross[:, span(i)]


def share_kernel(core_ref, sums_ref, share_ref, out_ref):
    parts = [share_ref[b, :, span(h)] for b in range(2) for h in range(2)]
    piece = jnp.concatenate(parts + [jnp.sum(sums_ref[...], axis=0)], axis=0)
    out_ref[...] = jnp.broadcast_to(piece[None], out_ref.shape)


def raw_block(parts_ref, b):
    rows = parts_ref.shape[0] * SUB
    halves = [
        parts_ref[:, SUB * (2 * b + h) : SUB * (2 * b + h + 1), :].reshape(rows, LANE) for h in range(2)
    ]
    return jnp.concatenate(halves, axis=1)


def inner_kernel(core_ref, parts_ref, own_ref, out_ref, *, count):
    pieces = out_ref.shape[0]
    own = own_ref[...]
    for b in range(2):
        gram = dot(raw_block(parts_ref, b), own, 0, 0) / count
        for h in range(2):
            part = gram[:, span(h)].reshape(pieces // 2, BASIS // 2, LANE)
            out_ref[span(b, pieces // 2), span(h, BASIS // 2), :] = part
    mine = jnp.where(core_ref[0] == 0, parts_ref[0, BASIS:, :], parts_ref[1, BASIS:, :])
    out_ref[:, BASIS:, :] = jnp.broadcast_to(mine[None], (pieces, GRAM, LANE))


def total_kernel(core_ref, parts_ref, mine_ref, out_ref):
    mine_ref[...] = parts_ref[:, BASIS:, :].reshape(mine_ref.shape)
    out_ref[...] = jnp.broadcast_to(jnp.sum(parts_ref[:, :BASIS, :], axis=0)[None], out_ref.shape)


def inverse_kernel(core_ref, mine_ref, other_ref, inv_ref, work_ref):
    n = inv_ref.shape[0]
    blocks = n // LANE
    first = core_ref[0] == 0
    work_ref[...] = jnp.zeros_like(work_ref)
    for half in range(2):
        for at, place in enumerate(HALVES[half]):
            if place is not None:
                mine, other = mine_ref[span(at), :], other_ref[span(at), :]
                tile = jnp.where(first == (half == 0), mine, other)
                work_ref[span(place[0]), span(place[1])] = tile
    for k in range(blocks):
        done = factor(work_ref[span(k), span(k)])
        row = lax.broadcasted_iota(jnp.int32, done.shape, 0)
        col = lax.broadcasted_iota(jnp.int32, done.shape, 1)
        done = jnp.where(row >= col, done, 0.0)
        work_ref[span(k), :] = dot(done, work_ref[span(k), :])
        work_ref[span(k), span(k)] = done
        for i in range(k + 1, blocks):
            up = work_ref[span(k), span(i)]
            work_ref[span(i), span(k)] = jnp.zeros((LANE, LANE), jnp.float32)
            work_ref[span(i), :] = work_ref[span(i), :] - dot(up, work_ref[span(k), :], 0, 0)
    for i in range(blocks):
        split = LANE * (i + 1)
        inv_ref[span(i), :split] = work_ref[span(i), :split]
        if split < n:
            inv_ref[span(i), split:] = jnp.zeros((LANE, n - split), jnp.float32)


def finish_kernel(index_ref, parts_ref, inv_ref, gram_ref, own_ref, out_ref):
    width = own_ref.shape[1]
    pieces = gram_ref.shape[0]
    index = index_ref[0]

    def basis(b):
        left = dot(raw_block(parts_ref, 0), inv_ref[span(b, width), :width], 1, 1)
        return left + dot(raw_block(parts_ref, 1), inv_ref[width:, width:], 1, 1) if b else left

    @pl.when(index == 0)
    def _():
        out_ref[...] = basis(0)

    @pl.when(index == 1)
    def _():
        out_ref[...] = basis(1)

    @pl.when(index > 1)
    def _():
        halves = [gram_ref[:, span(h, BASIS // 2), :].reshape(pieces * BASIS // 2, LANE) for h in range(2)]
        gram = jnp.concatenate(halves, axis=1)
        top = dot(inv_ref[:width, :width], gram[:width])
        low = dot(inv_ref[width:, :], gram)
        out_ref[...] = own_ref[...] - dot(basis(0), top) - dot(basis(1), low)


def swapped(pieces, axis):
    return lax.all_to_all(pieces, axis, 0, 0, tiled=True)


def on_device(own):
    rows, width = own.shape
    many, groups = lax.axis_size("row"), lax.axis_size("orb")
    count = rows * many
    index = lax.axis_index("orb")
    core = index % 2
    pairs = [(i, i ^ 1) for i in range(groups)]

    share = swapped(own.reshape(groups, -1, width), "orb")
    pair = lax.ppermute(own, "orb", pairs)
    half = call(
        functools.partial(half_kernel, count=count), [(many * GRAM, LANE)], core, own, pair, name="half"
    )[0]
    sums = swapped(half.reshape(many, GRAM, LANE), "row")
    parts = call(share_kernel, [(groups, BASIS + GRAM, LANE)], core, sums, share[:2], name="share")[0]
    parts = swapped(parts, "orb")
    inner = call(
        functools.partial(inner_kernel, count=count), [(many, BASIS + GRAM, LANE)], core, parts, own, name="inner"
    )[0]
    inner = swapped(inner, "row")
    mine, gram = call(
        total_kernel, [(many * GRAM, LANE), (many, BASIS, LANE)], core, inner, name="total"
    )
    gram = swapped(gram, "row")
    other = lax.ppermute(mine, "orb", pairs)
    inverse = call(
        inverse_kernel, [(2 * width, 2 * width)], core, mine, other, scratch=[(2 * width, 2 * width)], name="inverse"
    )[0]
    return call(finish_kernel, [own.shape], index, parts, inverse, gram, own, name="finish")[0]


def solution(mesh):
    return jax.shard_map(
        on_device,
        mesh=mesh,
        in_specs=(P("row", "orb"),),
        out_specs=P("row", "orb"),
        check_vma=False,
    )
```

```python
import functools

import jax
import jax.numpy as jnp
from jax import lax
from jax.experimental import pallas as pl
from jax.experimental.pallas import tpu as pltpu
from jax.sharding import PartitionSpec as P

SUB = 8
LANE = 128
EXACT = lax.Precision.HIGHEST


def dot(left, right, left_dim=1, right_dim=0):
    dims = (((left_dim,), (right_dim,)), ((), ()))
    return lax.dot_general(
        left, right, dims, precision=EXACT, preferred_element_type=jnp.float32
    )


NEAR = 2


def factor(block):
    shape = (SUB, LANE)
    lane = lax.broadcasted_iota(jnp.int32, shape, 1)
    sub = lax.broadcasted_iota(jnp.int32, shape, 0)
    count = LANE // SUB
    tiles = [block[SUB * t : SUB * (t + 1), :] for t in range(count)]

    def full(vector):
        return jnp.broadcast_to(vector, shape)

    def pick(vector, i):
        return jnp.take_along_axis(vector, jnp.full(shape, i, jnp.int32), axis=0)

    for k in range(count):
        base = SUB * k
        inside = (lane >= base) & (lane < base + SUB)
        own = tiles[k]
        columns = [full(own[:, base + j : base + j + 1]) for j in range(SUB)]
        diag = [[pick(columns[j], i) for j in range(i + 1)] for i in range(SUB)]
        root, low = [], [[None] * SUB for _ in range(SUB)]
        for j in range(SUB):
            root.append(lax.rsqrt(diag[j][j]))
            for i in range(j + 1, SUB):
                low[i][j] = diag[i][j] * root[j]
            for i in range(j + 1, SUB):
                for m in range(j + 1, i + 1):
                    diag[i][m] = diag[i][m] - low[i][j] * low[m][j]

        def solve(vectors):
            for j in range(SUB):
                vectors[j] = vectors[j] * root[j]
                for i in range(j + 1, SUB):
                    vectors[i] = vectors[i] - low[i][j] * vectors[j]
            return vectors

        cleared = jnp.where(inside, jnp.where(lane - base == sub, 1.0, 0.0), own)
        done = solve([full(cleared[i : i + 1, :]) for i in range(SUB)])
        row = done[0]
        for i in range(1, SUB):
            row = jnp.where(sub == i, done[i], row)
        tiles[k] = row
        if k + 1 + NEAR < count:
            flipped = jnp.transpose(row)
        for t in range(k + 1, count):
            if t <= k + NEAR:
                left = solve([full(tiles[t][:, base + j : base + j + 1]) for j in range(SUB)])
            else:
                left = [full(flipped[SUB * t : SUB * (t + 1), j : j + 1]) for j in range(SUB)]
            terms = [left[j] * done[j] for j in range(SUB)]
            while len(terms) > 1:
                terms = [terms[i] + terms[i + 1] for i in range(0, len(terms), 2)]
            tiles[t] = jnp.where(inside, 0.0, tiles[t]) - terms[0]
    return jnp.concatenate(tiles, axis=0)


def span(i, size=LANE):
    return slice(size * i, size * (i + 1))


HALVES = (((0, 0), (0, 1), None, (1, 1), (0, 2), (0, 3)), ((2, 2), (2, 3), None, (3, 3), (1, 2), (1, 3)))
GRAM = 24
BASIS = 32


def call(kernel, outs, scalar, *args, scratch=(), name):
    return pl.pallas_call(
        kernel,
        out_shape=[jax.ShapeDtypeStruct(shape, jnp.float32) for shape in outs],
        in_specs=[pl.BlockSpec(memory_space=pltpu.SMEM)] + [pl.BlockSpec(memory_space=pltpu.VMEM)] * len(args),
        out_specs=[pl.BlockSpec(memory_space=pltpu.VMEM)] * len(outs),
        scratch_shapes=[pltpu.VMEM(shape, jnp.float32) for shape in scratch],
        name=name,
    )(scalar.reshape(1), *args)


def half_kernel(core_ref, own_ref, pair_ref, half_ref, *, count):
    own, pair = own_ref[...], pair_ref[...]
    first = core_ref[0] == 0
    left = jnp.where(first, own[:, :LANE], pair[:, LANE:])
    right = jnp.where(first, pair, own)
    square = dot(own, own, 0, 0) / count
    cross = dot(left, right, 0, 0) / count
    for i in range(4):
        half_ref[span(i), :] = square[span(i // 2), span(i % 2)]
    for i in range(2):
        half_ref[span(4 + i), :] = cross[:, span(i)]


def share_kernel(core_ref, sums_ref, out_ref):
    out_ref[...] = jnp.broadcast_to(jnp.sum(sums_ref[...], axis=0)[None], out_ref.shape)


def raw_blocks(core, mine_ref, other_ref):
    mine, other = mine_ref[...], other_ref[...]
    return jnp.where(core == 0, mine, other), jnp.where(core == 0, other, mine)


def inner_kernel(core_ref, mine_ref, other_ref, gram_ref, own_ref, out_ref, *, count):
    pieces = out_ref.shape[0]
    own = own_ref[...]
    for b, block in enumerate(raw_blocks(core_ref[0], mine_ref, other_ref)):
        gram = dot(block, own, 0, 0) / count
        for h in range(2):
            part = gram[:, span(h)].reshape(pieces // 2, BASIS // 2, LANE)
            out_ref[span(b, pieces // 2), span(h, BASIS // 2), :] = part
    half = jnp.where(core_ref[0] == 0, gram_ref[0], gram_ref[1])
    out_ref[:, BASIS:, :] = jnp.broadcast_to(half[None], (pieces, GRAM, LANE))


def total_kernel(core_ref, parts_ref, mine_ref, out_ref):
    mine_ref[...] = parts_ref[:, BASIS:, :].reshape(mine_ref.shape)
    out_ref[...] = jnp.broadcast_to(jnp.sum(parts_ref[:, :BASIS, :], axis=0)[None], out_ref.shape)


def inverse_kernel(core_ref, mine_ref, other_ref, inv_ref, work_ref):
    n = inv_ref.shape[0]
    blocks = n // LANE
    first = core_ref[0] == 0
    work_ref[...] = jnp.zeros_like(work_ref)
    for half in range(2):
        for at, place in enumerate(HALVES[half]):
            if place is not None:
                mine, other = mine_ref[span(at), :], other_ref[span(at), :]
                tile = jnp.where(first == (half == 0), mine, other)
                work_ref[span(place[0]), span(place[1])] = tile
    for k in range(blocks):
        done = factor(work_ref[span(k), span(k)])
        row = lax.broadcasted_iota(jnp.int32, done.shape, 0)
        col = lax.broadcasted_iota(jnp.int32, done.shape, 1)
        done = jnp.where(row >= col, done, 0.0)
        work_ref[span(k), :] = dot(done, work_ref[span(k), :])
        work_ref[span(k), span(k)] = done
        for i in range(k + 1, blocks):
            up = work_ref[span(k), span(i)]
            work_ref[span(i), span(k)] = jnp.zeros((LANE, LANE), jnp.float32)
            work_ref[span(i), :] = work_ref[span(i), :] - dot(up, work_ref[span(k), :], 0, 0)
    for i in range(blocks):
        split = LANE * (i + 1)
        inv_ref[span(i), :split] = work_ref[span(i), :split]
        if split < n:
            inv_ref[span(i), split:] = jnp.zeros((LANE, n - split), jnp.float32)


def finish_kernel(index_ref, mine_ref, other_ref, inv_ref, gram_ref, own_ref, out_ref):
    width = own_ref.shape[1]
    pieces = gram_ref.shape[0]
    index = index_ref[0]
    zero, one = raw_blocks(index % 2, mine_ref, other_ref)

    def basis(b):
        left = dot(zero, inv_ref[span(b, width), :width], 1, 1)
        return left + dot(one, inv_ref[width:, width:], 1, 1) if b else left

    @pl.when(index == 0)
    def _():
        out_ref[...] = basis(0)

    @pl.when(index == 1)
    def _():
        out_ref[...] = basis(1)

    @pl.when(index > 1)
    def _():
        halves = [gram_ref[:, span(h, BASIS // 2), :].reshape(pieces * BASIS // 2, LANE) for h in range(2)]
        gram = jnp.concatenate(halves, axis=1)
        top = dot(inv_ref[:width, :width], gram[:width])
        low = dot(inv_ref[width:, :], gram)
        out_ref[...] = own_ref[...] - dot(basis(0), top) - dot(basis(1), low)


def swapped(pieces, axis):
    return lax.all_to_all(pieces, axis, 0, 0, tiled=True)


def steps(moves):
    return [(2 * source + c, 2 * target + c) for source, target in moves for c in range(2)]


def on_device(own):
    rows, width = own.shape
    many, groups = lax.axis_size("row"), lax.axis_size("orb")
    count = rows * many
    index = lax.axis_index("orb")
    core, chip = index % 2, index // 2
    pairs = [(i, i ^ 1) for i in range(groups)]

    pair = lax.ppermute(own, "orb", pairs)
    first = lax.ppermute(own, "orb", steps([(0, 3)])) + lax.ppermute(own, "orb", steps([(0, 5)]))
    first = jnp.where(chip == 0, own, first)
    mine = first + lax.ppermute(first, "orb", steps([(0, 1), (3, 4), (5, 6)]))
    mine = mine + lax.ppermute(first, "orb", steps([(0, 7), (3, 2)]))
    other = lax.ppermute(mine, "orb", pairs)

    half = call(
        functools.partial(half_kernel, count=count), [(many * GRAM, LANE)], core, own, pair, name="half"
    )[0]
    sums = swapped(half.reshape(many, GRAM, LANE), "row")
    half = call(share_kernel, [(groups, GRAM, LANE)], core, sums, name="share")[0]
    half = swapped(half, "orb")[:2]
    inner = call(
        functools.partial(inner_kernel, count=count),
        [(many, BASIS + GRAM, LANE)], core, mine, other, half, own, name="inner",
    )[0]
    inner = swapped(inner, "row")
    tiles, gram = call(
        total_kernel, [(many * GRAM, LANE), (many, BASIS, LANE)], core, inner, name="total"
    )
    gram = swapped(gram, "row")
    inverse = call(
        inverse_kernel, [(2 * width, 2 * width)], core, tiles, lax.ppermute(tiles, "orb", pairs),
        scratch=[(2 * width, 2 * width)], name="inverse",
    )[0]
    return call(finish_kernel, [own.shape], index, mine, other, inverse, gram, own, name="finish")[0]


def solution(mesh):
    return jax.shard_map(
        on_device,
        mesh=mesh,
        in_specs=(P("row", "orb"),),
        out_specs=P("row", "orb"),
        check_vma=False,
    )
```

```python
import functools

import jax
import jax.numpy as jnp
from jax import lax
from jax.experimental import pallas as pl
from jax.experimental.pallas import tpu as pltpu
from jax.sharding import PartitionSpec as P


SUB = 8
LANE = 128
EXACT = lax.Precision.HIGHEST


def dot(left, right, left_dim=1, right_dim=0):
    dims = (((left_dim,), (right_dim,)), ((), ()))
    return lax.dot_general(
        left, right, dims, precision=EXACT, preferred_element_type=jnp.float32
    )


NEAR = 2


def factor(block):
    shape = (SUB, LANE)
    lane = lax.broadcasted_iota(jnp.int32, shape, 1)
    sub = lax.broadcasted_iota(jnp.int32, shape, 0)
    count = LANE // SUB
    tiles = [block[SUB * t : SUB * (t + 1), :] for t in range(count)]

    def full(vector):
        return jnp.broadcast_to(vector, shape)

    def pick(vector, i):
        return jnp.take_along_axis(vector, jnp.full(shape, i, jnp.int32), axis=0)

    for k in range(count):
        base = SUB * k
        inside = (lane >= base) & (lane < base + SUB)
        own = tiles[k]
        columns = [full(own[:, base + j : base + j + 1]) for j in range(SUB)]
        diag = [[pick(columns[j], i) for j in range(i + 1)] for i in range(SUB)]
        root, low = [], [[None] * SUB for _ in range(SUB)]
        for j in range(SUB):
            root.append(lax.rsqrt(diag[j][j]))
            for i in range(j + 1, SUB):
                low[i][j] = diag[i][j] * root[j]
            for i in range(j + 1, SUB):
                for m in range(j + 1, i + 1):
                    diag[i][m] = diag[i][m] - low[i][j] * low[m][j]

        def solve(vectors):
            for j in range(SUB):
                vectors[j] = vectors[j] * root[j]
                for i in range(j + 1, SUB):
                    vectors[i] = vectors[i] - low[i][j] * vectors[j]
            return vectors

        cleared = jnp.where(inside, jnp.where(lane - base == sub, 1.0, 0.0), own)
        done = solve([full(cleared[i : i + 1, :]) for i in range(SUB)])
        row = done[0]
        for i in range(1, SUB):
            row = jnp.where(sub == i, done[i], row)
        tiles[k] = row
        if k + 1 + NEAR < count:
            flipped = jnp.transpose(row)
        for t in range(k + 1, count):
            if t <= k + NEAR:
                left = solve([full(tiles[t][:, base + j : base + j + 1]) for j in range(SUB)])
            else:
                left = [full(flipped[SUB * t : SUB * (t + 1), j : j + 1]) for j in range(SUB)]
            terms = [left[j] * done[j] for j in range(SUB)]
            while len(terms) > 1:
                terms = [terms[i] + terms[i + 1] for i in range(0, len(terms), 2)]
            tiles[t] = jnp.where(inside, 0.0, tiles[t]) - terms[0]
    return jnp.concatenate(tiles, axis=0)


def span(i, size=LANE):
    return slice(size * i, size * (i + 1))


HALVES = (((0, 0), (0, 1), None, (1, 1), (0, 2), (0, 3)), ((2, 2), (2, 3), None, (3, 3), (1, 2), (1, 3)))
GRAM = 24
BASIS = 32


def call(kernel, outs, scalar, *args, scratch=()):
    return pl.pallas_call(
        kernel,
        out_shape=[jax.ShapeDtypeStruct(shape, jnp.float32) for shape in outs],
        in_specs=[pl.BlockSpec(memory_space=pltpu.SMEM)] + [pl.BlockSpec(memory_space=pltpu.VMEM)] * len(args),
        out_specs=[pl.BlockSpec(memory_space=pltpu.VMEM)] * len(outs),
        scratch_shapes=[pltpu.VMEM(shape, jnp.float32) for shape in scratch],
    )(scalar.reshape(1), *args)


def raw_blocks(core, mine_ref, other_ref):
    mine, other = mine_ref[...], other_ref[...]
    return jnp.where(core == 0, mine, other), jnp.where(core == 0, other, mine)


def inner_kernel(core_ref, mine_ref, other_ref, own_ref, out_ref, *, count):
    pieces = out_ref.shape[0]
    mine, other, own = mine_ref[...], other_ref[...], own_ref[...]
    first = core_ref[0] == 0
    for b, block in enumerate(raw_blocks(core_ref[0], mine_ref, other_ref)):
        gram = dot(block, own, 0, 0) / count
        for h in range(2):
            part = gram[:, span(h)].reshape(pieces // 2, BASIS // 2, LANE)
            out_ref[span(b, pieces // 2), span(h, BASIS // 2), :] = part
    square = dot(mine, mine, 0, 0) / count
    left = jnp.where(first, mine[:, :LANE], other[:, LANE:])
    cross = dot(left, jnp.where(first, other, mine), 0, 0) / count
    tiles = [square[span(i // 2), span(i % 2)] for i in range(4)] + [cross[:, span(i)] for i in range(2)]
    out_ref[:, BASIS:, :] = jnp.concatenate(tiles, axis=0).reshape(pieces, GRAM, LANE)


def total_kernel(core_ref, parts_ref, tiles_ref, out_ref):
    total = jnp.sum(parts_ref[...], axis=0)
    tiles_ref[...] = jnp.broadcast_to(total[None, BASIS:], tiles_ref.shape)
    out_ref[...] = jnp.broadcast_to(total[None, :BASIS], out_ref.shape)


def inverse_kernel(core_ref, mine_ref, other_ref, inv_ref, work_ref):
    n = inv_ref.shape[0]
    blocks = n // LANE
    first = core_ref[0] == 0
    work_ref[...] = jnp.zeros_like(work_ref)
    for half in range(2):
        for at, place in enumerate(HALVES[half]):
            if place is not None:
                mine, other = mine_ref[span(at), :], other_ref[span(at), :]
                tile = jnp.where(first == (half == 0), mine, other)
                work_ref[span(place[0]), span(place[1])] = tile
    for k in range(blocks):
        done = factor(work_ref[span(k), span(k)])
        row = lax.broadcasted_iota(jnp.int32, done.shape, 0)
        col = lax.broadcasted_iota(jnp.int32, done.shape, 1)
        done = jnp.where(row >= col, done, 0.0)
        work_ref[span(k), :] = dot(done, work_ref[span(k), :])
        work_ref[span(k), span(k)] = done
        for i in range(k + 1, blocks):
            up = work_ref[span(k), span(i)]
            work_ref[span(i), span(k)] = jnp.zeros((LANE, LANE), jnp.float32)
            work_ref[span(i), :] = work_ref[span(i), :] - dot(up, work_ref[span(k), :], 0, 0)
    for i in range(blocks):
        split = LANE * (i + 1)
        inv_ref[span(i), :split] = work_ref[span(i), :split]
        if split < n:
            inv_ref[span(i), split:] = jnp.zeros((LANE, n - split), jnp.float32)


def finish_kernel(index_ref, mine_ref, other_ref, inv_ref, gram_ref, own_ref, out_ref):
    width = own_ref.shape[1]
    pieces = gram_ref.shape[0]
    index = index_ref[0]
    zero, one = raw_blocks(index % 2, mine_ref, other_ref)

    def basis(b):
        left = dot(zero, inv_ref[span(b, width), :width], 1, 1)
        return left + dot(one, inv_ref[width:, width:], 1, 1) if b else left

    @pl.when(index == 0)
    def _():
        out_ref[...] = basis(0)

    @pl.when(index == 1)
    def _():
        out_ref[...] = basis(1)

    @pl.when(index > 1)
    def _():
        halves = [gram_ref[:, span(h, BASIS // 2), :].reshape(pieces * BASIS // 2, LANE) for h in range(2)]
        gram = jnp.concatenate(halves, axis=1)
        top = dot(inv_ref[:width, :width], gram[:width])
        low = dot(inv_ref[width:, :], gram)
        out_ref[...] = own_ref[...] - dot(basis(0), top) - dot(basis(1), low)


def swapped(pieces, axis):
    return lax.all_to_all(pieces, axis, 0, 0, tiled=True)


def steps(moves):
    return [(2 * source + c, 2 * target + c) for source, target in moves for c in range(2)]


def on_device(own):
    rows, width = own.shape
    many, groups = lax.axis_size("row"), lax.axis_size("orb")
    count = rows * many
    index = lax.axis_index("orb")
    core, chip = index % 2, index // 2
    pairs = [(i, i ^ 1) for i in range(groups)]

    first = lax.ppermute(own, "orb", steps([(0, 3)])) + lax.ppermute(own, "orb", steps([(0, 5)]))
    first = jnp.where(chip == 0, own, first)
    mine = first + lax.ppermute(first, "orb", steps([(0, 1), (3, 4), (5, 6)]))
    mine = mine + lax.ppermute(first, "orb", steps([(0, 7), (3, 2)]))
    other = lax.ppermute(mine, "orb", pairs)

    inner = call(functools.partial(inner_kernel, count=count), [(many, BASIS + GRAM, LANE)], core, mine, other, own)[0]
    tiles, gram = call(total_kernel, [(many, GRAM, LANE), (many, BASIS, LANE)], core, swapped(inner, "row"))
    tiles, gram = lax.optimization_barrier((swapped(tiles, "row").reshape(-1, LANE), gram))
    gram = swapped(gram, "row")
    others = lax.ppermute(tiles, "orb", pairs)
    inverse = call(
        inverse_kernel, [(2 * width, 2 * width)], core, tiles, others,
        scratch=[(2 * width, 2 * width)],
    )[0]
    return call(finish_kernel, [own.shape], index, mine, other, inverse, gram, own)[0]


def solution(mesh):
    return jax.shard_map(
        on_device,
        mesh=mesh,
        in_specs=(P("row", "orb"),),
        out_specs=P("row", "orb"),
        check_vma=False,
    )
```

```python
import functools

import jax
import jax.numpy as jnp
from jax import lax
from jax.experimental import pallas as pl
from jax.experimental.pallas import tpu as pltpu
from jax.sharding import PartitionSpec as P


SUB = 8
LANE = 128
EXACT = lax.Precision.HIGHEST


def dot(left, right, left_dim=1, right_dim=0):
    dims = (((left_dim,), (right_dim,)), ((), ()))
    return lax.dot_general(
        left, right, dims, precision=EXACT, preferred_element_type=jnp.float32
    )


NEAR = 2


def factor(block):
    shape = (SUB, LANE)
    lane = lax.broadcasted_iota(jnp.int32, shape, 1)
    sub = lax.broadcasted_iota(jnp.int32, shape, 0)
    count = LANE // SUB
    tiles = [block[SUB * t : SUB * (t + 1), :] for t in range(count)]

    def full(vector):
        return jnp.broadcast_to(vector, shape)

    def pick(vector, i):
        return jnp.take_along_axis(vector, jnp.full(shape, i, jnp.int32), axis=0)

    for k in range(count):
        base = SUB * k
        inside = (lane >= base) & (lane < base + SUB)
        own = tiles[k]
        columns = [full(own[:, base + j : base + j + 1]) for j in range(SUB)]
        diag = [[pick(columns[j], i) for j in range(i + 1)] for i in range(SUB)]
        root, low = [], [[None] * SUB for _ in range(SUB)]
        for j in range(SUB):
            root.append(lax.rsqrt(diag[j][j]))
            for i in range(j + 1, SUB):
                low[i][j] = diag[i][j] * root[j]
            for i in range(j + 1, SUB):
                for m in range(j + 1, i + 1):
                    diag[i][m] = diag[i][m] - low[i][j] * low[m][j]

        def solve(vectors):
            for j in range(SUB):
                vectors[j] = vectors[j] * root[j]
                for i in range(j + 1, SUB):
                    vectors[i] = vectors[i] - low[i][j] * vectors[j]
            return vectors

        cleared = jnp.where(inside, jnp.where(lane - base == sub, 1.0, 0.0), own)
        done = solve([full(cleared[i : i + 1, :]) for i in range(SUB)])
        row = done[0]
        for i in range(1, SUB):
            row = jnp.where(sub == i, done[i], row)
        tiles[k] = row
        near = range(k + 1, min(k + 1 + NEAR, count))
        far = range(k + 1 + NEAR, count)
        raws = [[full(tiles[t][:, base + j : base + j + 1]) for t in near] for j in range(SUB)]
        for i, t in enumerate(near):
            left = solve([raws[j][i] for j in range(SUB)])
            terms = [left[j] * done[j] for j in range(SUB)]
            while len(terms) > 1:
                terms = [terms[m] + terms[m + 1] for m in range(0, len(terms), 2)]
            tiles[t] = jnp.where(inside, 0.0, tiles[t]) - terms[0]
        if far:
            top = row.astype(jnp.bfloat16).astype(jnp.float32)
            mid = (row - top).astype(jnp.bfloat16).astype(jnp.float32)
            end = row - top - mid
            left = jnp.concatenate([top, top, mid, mid, top, end], axis=0).astype(jnp.bfloat16)
            right = jnp.concatenate([top, mid, top, mid, end, top], axis=0).astype(jnp.bfloat16)
            terms = lax.dot_general(left, right, (((0,), (0,)), ((), ())), preferred_element_type=jnp.float32)
            for t in far:
                tiles[t] = jnp.where(inside, 0.0, tiles[t]) - terms[span(t, SUB), :]
    return jnp.concatenate(tiles, axis=0)


def span(i, size=LANE):
    return slice(size * i, size * (i + 1))


HALVES = (((0, 0), (0, 1), None, (1, 1), (0, 2), (0, 3)), ((2, 2), (2, 3), None, (3, 3), (1, 2), (1, 3)))
GRAM = 24
BASIS = 32


def call(kernel, outs, scalar, *args, scratch=(), near=False):
    kind = pltpu.VMEM if near else jax.ShapeDtypeStruct
    return pl.pallas_call(
        kernel,
        out_shape=[kind(shape, jnp.float32) for shape in outs],
        in_specs=[pl.BlockSpec(memory_space=pltpu.SMEM)] + [pl.BlockSpec(memory_space=pltpu.VMEM)] * len(args),
        out_specs=[pl.BlockSpec(memory_space=pltpu.VMEM)] * len(outs),
        scratch_shapes=[pltpu.VMEM(shape, jnp.float32) for shape in scratch],
    )(scalar.reshape(1), *[pltpu.with_memory_space_constraint(a, pltpu.VMEM) for a in args])


def raw_blocks(core, mine_ref, other_ref):
    mine, other = mine_ref[...], other_ref[...]
    return jnp.where(core == 0, mine, other), jnp.where(core == 0, other, mine)


def inner_kernel(core_ref, mine_ref, other_ref, own_ref, out_ref, *, count):
    pieces = out_ref.shape[0]
    mine, other, own = mine_ref[...], other_ref[...], own_ref[...]
    first = core_ref[0] == 0
    for b, block in enumerate(raw_blocks(core_ref[0], mine_ref, other_ref)):
        gram = dot(block, own, 0, 0) / count
        for h in range(2):
            part = gram[:, span(h)].reshape(pieces // 2, BASIS // 2, LANE)
            out_ref[span(b, pieces // 2), span(h, BASIS // 2), :] = part
    square = dot(mine, mine, 0, 0) / count
    left = jnp.where(first, mine[:, :LANE], other[:, LANE:])
    cross = dot(left, jnp.where(first, other, mine), 0, 0) / count
    tiles = [square[span(i // 2), span(i % 2)] for i in range(4)] + [cross[:, span(i)] for i in range(2)]
    out_ref[:, BASIS:, :] = jnp.concatenate(tiles, axis=0).reshape(pieces, GRAM, LANE)


def total_kernel(core_ref, parts_ref, tiles_ref, out_ref):
    total = jnp.sum(parts_ref[...], axis=0)
    tiles_ref[...] = jnp.broadcast_to(total[None, BASIS:], tiles_ref.shape)
    out_ref[...] = jnp.broadcast_to(total[None, :BASIS], out_ref.shape)


def inverse_kernel(core_ref, mine_ref, other_ref, inv_ref, work_ref):
    n = inv_ref.shape[0]
    blocks = n // LANE
    first = core_ref[0] == 0
    work_ref[...] = jnp.zeros_like(work_ref)
    for half in range(2):
        for at, place in enumerate(HALVES[half]):
            if place is not None:
                mine, other = mine_ref[span(at), :], other_ref[span(at), :]
                tile = jnp.where(first == (half == 0), mine, other)
                work_ref[span(place[0]), span(place[1])] = tile
    for k in range(blocks):
        done = factor(work_ref[span(k), span(k)])
        row = lax.broadcasted_iota(jnp.int32, done.shape, 0)
        col = lax.broadcasted_iota(jnp.int32, done.shape, 1)
        done = jnp.where(row >= col, done, 0.0)
        work_ref[span(k), :] = dot(done, work_ref[span(k), :])
        work_ref[span(k), span(k)] = done
        for i in range(k + 1, blocks):
            up = work_ref[span(k), span(i)]
            work_ref[span(i), span(k)] = jnp.zeros((LANE, LANE), jnp.float32)
            work_ref[span(i), :] = work_ref[span(i), :] - dot(up, work_ref[span(k), :], 0, 0)
    for i in range(blocks):
        split = LANE * (i + 1)
        inv_ref[span(i), :split] = work_ref[span(i), :split]
        if split < n:
            inv_ref[span(i), split:] = jnp.zeros((LANE, n - split), jnp.float32)


def basis_kernel(core_ref, mine_ref, other_ref, inv_ref, basis_ref):
    zero, one = raw_blocks(core_ref[0], mine_ref, other_ref)
    width = zero.shape[1]
    basis_ref[:, :width] = dot(zero, inv_ref[:width, :width], 1, 1)
    low = dot(zero, inv_ref[width:, :width], 1, 1)
    basis_ref[:, width:] = low + dot(one, inv_ref[width:, width:], 1, 1)


def finish_kernel(index_ref, basis_ref, inv_ref, gram_ref, own_ref, out_ref):
    width = own_ref.shape[1]
    pieces = gram_ref.shape[0]
    index = index_ref[0]

    @pl.when(index == 0)
    def _():
        out_ref[...] = basis_ref[:, :width]

    @pl.when(index == 1)
    def _():
        out_ref[...] = basis_ref[:, width:]

    @pl.when(index > 1)
    def _():
        halves = [gram_ref[:, span(h, BASIS // 2), :].reshape(pieces * BASIS // 2, LANE) for h in range(2)]
        gram = jnp.concatenate(halves, axis=1)
        top = dot(inv_ref[:width, :width], gram[:width])
        low = dot(inv_ref[width:, :], gram)
        out_ref[...] = own_ref[...] - dot(basis_ref[:, :width], top) - dot(basis_ref[:, width:], low)


def swapped(pieces, axis):
    return lax.all_to_all(pieces, axis, 0, 0, tiled=True)


def steps(moves):
    return [(2 * source + c, 2 * target + c) for source, target in moves for c in range(2)]


def on_device(own):
    rows, width = own.shape
    many, groups = lax.axis_size("row"), lax.axis_size("orb")
    count = rows * many
    index = lax.axis_index("orb")
    core, chip = index % 2, index // 2
    pairs = [(i, i ^ 1) for i in range(groups)]

    first = lax.ppermute(own, "orb", steps([(0, 3)])) + lax.ppermute(own, "orb", steps([(0, 5)]))
    first = jnp.where(chip == 0, own, first)
    mine = first + lax.ppermute(first, "orb", steps([(0, 1), (3, 4), (5, 6)]))
    mine = mine + lax.ppermute(first, "orb", steps([(0, 7), (3, 2)]))
    other = lax.ppermute(mine, "orb", pairs)

    inner = call(functools.partial(inner_kernel, count=count), [(many, BASIS + GRAM, LANE)], core, mine, other, own)[0]
    tiles, gram = call(total_kernel, [(many, GRAM, LANE), (many, BASIS, LANE)], core, swapped(inner, "row"))
    tiles, gram = lax.optimization_barrier((swapped(tiles, "row").reshape(-1, LANE), gram))
    gram = swapped(gram, "row")
    others = lax.ppermute(tiles, "orb", pairs)
    inverse = call(
        inverse_kernel, [(2 * width, 2 * width)], core, tiles, others,
        scratch=[(2 * width, 2 * width)], near=True,
    )[0]
    basis = call(basis_kernel, [(rows, 2 * width)], core, mine, other, inverse, near=True)[0]
    return call(finish_kernel, [own.shape], index, basis, inverse, gram, own)[0]


def solution(mesh):
    return jax.shard_map(
        on_device,
        mesh=mesh,
        in_specs=(P("row", "orb"),),
        out_specs=P("row", "orb"),
        check_vma=False,
    )
```

```python
import functools

import jax
import jax.numpy as jnp
from jax import lax
from jax.experimental import pallas as pl
from jax.experimental.pallas import tpu as pltpu
from jax.sharding import PartitionSpec as P


SUB = 8
LANE = 128
EXACT = lax.Precision.HIGHEST


def dot(left, right, left_dim=1, right_dim=0):
    dims = (((left_dim,), (right_dim,)), ((), ()))
    return lax.dot_general(
        left, right, dims, precision=EXACT, preferred_element_type=jnp.float32
    )


NEAR = 2


def factor(block):
    shape = (SUB, LANE)
    lane = lax.broadcasted_iota(jnp.int32, shape, 1)
    sub = lax.broadcasted_iota(jnp.int32, shape, 0)
    count = LANE // SUB
    tiles = [block[SUB * t : SUB * (t + 1), :] for t in range(count)]

    def full(vector):
        return jnp.broadcast_to(vector, shape)

    def pick(vector, i):
        return jnp.take_along_axis(vector, jnp.full(shape, i, jnp.int32), axis=0)

    for k in range(count):
        base = SUB * k
        inside = (lane >= base) & (lane < base + SUB)
        own = tiles[k]
        columns = [full(own[:, base + j : base + j + 1]) for j in range(SUB)]
        diag = [[pick(columns[j], i) for j in range(i + 1)] for i in range(SUB)]
        root, low = [], [[None] * SUB for _ in range(SUB)]
        for j in range(SUB):
            root.append(lax.rsqrt(diag[j][j]))
            for i in range(j + 1, SUB):
                low[i][j] = diag[i][j] * root[j]
            for i in range(j + 1, SUB):
                for m in range(j + 1, i + 1):
                    diag[i][m] = diag[i][m] - low[i][j] * low[m][j]

        def solve(vectors):
            for j in range(SUB):
                vectors[j] = vectors[j] * root[j]
                for i in range(j + 1, SUB):
                    vectors[i] = vectors[i] - low[i][j] * vectors[j]
            return vectors

        cleared = jnp.where(inside, jnp.where(lane - base == sub, 1.0, 0.0), own)
        done = solve([full(cleared[i : i + 1, :]) for i in range(SUB)])
        row = done[0]
        for i in range(1, SUB):
            row = jnp.where(sub == i, done[i], row)
        tiles[k] = row
        near = range(k + 1, min(k + 1 + NEAR, count))
        far = range(k + 1 + NEAR, count)
        raws = [[full(tiles[t][:, base + j : base + j + 1]) for t in near] for j in range(SUB)]
        for i, t in enumerate(near):
            left = solve([raws[j][i] for j in range(SUB)])
            terms = [left[j] * done[j] for j in range(SUB)]
            while len(terms) > 1:
                terms = [terms[m] + terms[m + 1] for m in range(0, len(terms), 2)]
            tiles[t] = jnp.where(inside, 0.0, tiles[t]) - terms[0]
        if far:
            top = row.astype(jnp.bfloat16).astype(jnp.float32)
            mid = (row - top).astype(jnp.bfloat16).astype(jnp.float32)
            end = row - top - mid
            left = jnp.concatenate([top, top, mid, mid, top, end], axis=0).astype(jnp.bfloat16)
            right = jnp.concatenate([top, mid, top, mid, end, top], axis=0).astype(jnp.bfloat16)
            terms = lax.dot_general(left, right, (((0,), (0,)), ((), ())), preferred_element_type=jnp.float32)
            for t in far:
                tiles[t] = jnp.where(inside, 0.0, tiles[t]) - terms[span(t, SUB), :]
    return jnp.concatenate(tiles, axis=0)


def span(i, size=LANE):
    return slice(size * i, size * (i + 1))


HALVES = (((0, 0), (0, 1), None, (1, 1), (0, 2), (0, 3)), ((2, 2), (2, 3), None, (3, 3), (1, 2), (1, 3)))
GRAM = 24
BASIS = 32


def call(kernel, outs, scalar, *args, scratch=(), near=(True,)):
    kinds = [pltpu.VMEM if here else jax.ShapeDtypeStruct for here in near]
    return pl.pallas_call(
        kernel,
        out_shape=[kind(shape, jnp.float32) for kind, shape in zip(kinds, outs)],
        in_specs=[pl.BlockSpec(memory_space=pltpu.SMEM)] + [pl.BlockSpec(memory_space=pltpu.VMEM)] * len(args),
        out_specs=[pl.BlockSpec(memory_space=pltpu.VMEM)] * len(outs),
        scratch_shapes=[pltpu.VMEM(shape, jnp.float32) for shape in scratch],
    )(scalar.reshape(1), *[pltpu.with_memory_space_constraint(a, pltpu.VMEM) for a in args])


def raw_blocks(core, mine_ref, other_ref):
    mine, other = mine_ref[...], other_ref[...]
    return jnp.where(core == 0, mine, other), jnp.where(core == 0, other, mine)


def inner_kernel(core_ref, mine_ref, other_ref, own_ref, out_ref, *, count):
    pieces = out_ref.shape[0]
    mine, other, own = mine_ref[...], other_ref[...], own_ref[...]
    first = core_ref[0] == 0
    for b, block in enumerate(raw_blocks(core_ref[0], mine_ref, other_ref)):
        gram = dot(block, own, 0, 0) / count
        for h in range(2):
            part = gram[:, span(h)].reshape(pieces // 2, BASIS // 2, LANE)
            out_ref[span(b, pieces // 2), span(h, BASIS // 2), :] = part
    square = dot(mine, mine, 0, 0) / count
    left = jnp.where(first, mine[:, :LANE], other[:, LANE:])
    cross = dot(left, jnp.where(first, other, mine), 0, 0) / count
    tiles = [square[span(i // 2), span(i % 2)] for i in range(4)] + [cross[:, span(i)] for i in range(2)]
    out_ref[:, BASIS:, :] = jnp.concatenate(tiles, axis=0).reshape(pieces, GRAM, LANE)


def total_kernel(core_ref, parts_ref, tiles_ref, out_ref):
    total = jnp.sum(parts_ref[...], axis=0)
    tiles_ref[...] = jnp.broadcast_to(total[None, BASIS:], tiles_ref.shape)
    out_ref[...] = jnp.broadcast_to(total[None, :BASIS], out_ref.shape)


def inverse_kernel(core_ref, mine_ref, other_ref, inv_ref, work_ref):
    n = inv_ref.shape[0]
    blocks = n // LANE
    first = core_ref[0] == 0
    work_ref[...] = jnp.zeros_like(work_ref)
    for half in range(2):
        for at, place in enumerate(HALVES[half]):
            if place is not None:
                mine, other = mine_ref[span(at), :], other_ref[span(at), :]
                tile = jnp.where(first == (half == 0), mine, other)
                work_ref[span(place[0]), span(place[1])] = tile
    for k in range(blocks):
        done = factor(work_ref[span(k), span(k)])
        row = lax.broadcasted_iota(jnp.int32, done.shape, 0)
        col = lax.broadcasted_iota(jnp.int32, done.shape, 1)
        done = jnp.where(row >= col, done, 0.0)
        sides = [slice(0, LANE * k), slice(LANE * (k + 1), n)]
        for side in sides:
            if side.start < side.stop:
                work_ref[span(k), side] = dot(done, work_ref[span(k), side])
        work_ref[span(k), span(k)] = done
        for i in range(k + 1, blocks):
            up = work_ref[span(k), span(i)]
            work_ref[span(i), span(k)] = jnp.zeros((LANE, LANE), jnp.float32)
            for side in (slice(LANE * i, n), slice(0, LANE * (k + 1))):
                work_ref[span(i), side] = work_ref[span(i), side] - dot(up, work_ref[span(k), side], 0, 0)
    for i in range(blocks):
        split = LANE * (i + 1)
        inv_ref[span(i), :split] = work_ref[span(i), :split]
        if split < n:
            inv_ref[span(i), split:] = jnp.zeros((LANE, n - split), jnp.float32)


def basis_kernel(index_ref, mine_ref, other_ref, inv_ref, basis_ref):
    zero, one = raw_blocks(index_ref[0] % 2, mine_ref, other_ref)
    width = zero.shape[1]
    top = dot(zero, inv_ref[:width, :width], 1, 1)
    low = dot(zero, inv_ref[width:, :width], 1, 1) + dot(one, inv_ref[width:, width:], 1, 1)
    basis_ref[:, :width] = jnp.where(index_ref[0] == 1, low, top)
    basis_ref[:, width:] = low

    @pl.when(index_ref[0] > 1)
    def _():
        basis_ref[:, :width] = dot(top, inv_ref[:width, :width]) + dot(low, inv_ref[width:, :width])
        basis_ref[:, width:] = dot(low, inv_ref[width:, width:])


def finish_kernel(index_ref, basis_ref, gram_ref, own_ref, out_ref):
    width = own_ref.shape[1]
    pieces = gram_ref.shape[0]

    @pl.when(index_ref[0] < 2)
    def _():
        out_ref[...] = basis_ref[:, :width]

    @pl.when(index_ref[0] > 1)
    def _():
        for h in range(2):
            gram = gram_ref[:, span(h, BASIS // 2), :].reshape(pieces * BASIS // 2, LANE)
            out_ref[:, span(h)] = own_ref[:, span(h)] - dot(basis_ref[...], gram)


def swapped(pieces, axis):
    return lax.all_to_all(pieces, axis, 0, 0, tiled=True)


def steps(moves):
    return [(2 * source + c, 2 * target + c) for source, target in moves for c in range(2)]


def on_device(own):
    rows, width = own.shape
    many, groups = lax.axis_size("row"), lax.axis_size("orb")
    count = rows * many
    index = lax.axis_index("orb")
    core, chip = index % 2, index // 2
    pairs = [(i, i ^ 1) for i in range(groups)]

    first = lax.ppermute(own, "orb", steps([(0, 3)])) + lax.ppermute(own, "orb", steps([(0, 5)]))
    first = jnp.where(chip == 0, own, first)
    mine = first + lax.ppermute(first, "orb", steps([(0, 1), (3, 4), (5, 6)]))
    mine = mine + lax.ppermute(first, "orb", steps([(0, 7), (3, 2)]))
    other = lax.ppermute(mine, "orb", pairs)

    inner = call(functools.partial(inner_kernel, count=count), [(many, BASIS + GRAM, LANE)], core, mine, other, own)[0]
    tiles, gram = call(
        total_kernel, [(many, GRAM, LANE), (many, BASIS, LANE)], core, swapped(inner, "row"),
        near=(True, False),
    )
    tiles, gram = lax.optimization_barrier((swapped(tiles, "row").reshape(-1, LANE), gram))
    gram = swapped(gram, "row")
    others = lax.ppermute(tiles, "orb", pairs)
    inverse = call(
        inverse_kernel, [(2 * width, 2 * width)], core, tiles, others,
        scratch=[(2 * width, 2 * width)],
    )[0]
    basis = call(basis_kernel, [(rows, 2 * width)], index, mine, other, inverse)[0]
    return call(finish_kernel, [own.shape], index, basis, gram, own, near=(False,))[0]


def solution(mesh):
    return jax.shard_map(
        on_device,
        mesh=mesh,
        in_specs=(P("row", "orb"),),
        out_specs=P("row", "orb"),
        check_vma=False,
    )
```

```python
import functools

import jax
import jax.numpy as jnp
from jax import lax
from jax.experimental import pallas as pl
from jax.experimental.pallas import tpu as pltpu
from jax.sharding import PartitionSpec as P


SUB = 8
LANE = 128
EXACT = lax.Precision.HIGHEST


def dot(left, right, left_dim=1, right_dim=0):
    dims = (((left_dim,), (right_dim,)), ((), ()))
    return lax.dot_general(
        left, right, dims, precision=EXACT, preferred_element_type=jnp.float32
    )


NEAR = 2


def factor(block):
    shape = (SUB, LANE)
    lane = lax.broadcasted_iota(jnp.int32, shape, 1)
    sub = lax.broadcasted_iota(jnp.int32, shape, 0)
    count = LANE // SUB
    tiles = [block[SUB * t : SUB * (t + 1), :] for t in range(count)]

    def full(vector):
        return jnp.broadcast_to(vector, shape)

    def pick(vector, i):
        return jnp.take_along_axis(vector, jnp.full(shape, i, jnp.int32), axis=0)

    for k in range(count):
        base = SUB * k
        inside = (lane >= base) & (lane < base + SUB)
        own = tiles[k]
        columns = [full(own[:, base + j : base + j + 1]) for j in range(SUB)]
        diag = [[pick(columns[j], i) for j in range(i + 1)] for i in range(SUB)]
        root, low = [], [[None] * SUB for _ in range(SUB)]
        for j in range(SUB):
            root.append(lax.rsqrt(diag[j][j]))
            for i in range(j + 1, SUB):
                low[i][j] = diag[i][j] * root[j]
            for i in range(j + 1, SUB):
                for m in range(j + 1, i + 1):
                    diag[i][m] = diag[i][m] - low[i][j] * low[m][j]

        def solve(vectors):
            for j in range(SUB):
                vectors[j] = vectors[j] * root[j]
                for i in range(j + 1, SUB):
                    vectors[i] = vectors[i] - low[i][j] * vectors[j]
            return vectors

        cleared = jnp.where(inside, jnp.where(lane - base == sub, 1.0, 0.0), own)
        done = solve([full(cleared[i : i + 1, :]) for i in range(SUB)])
        row = done[0]
        for i in range(1, SUB):
            row = jnp.where(sub == i, done[i], row)
        tiles[k] = row
        near = range(k + 1, min(k + 1 + NEAR, count))
        far = range(k + 1 + NEAR, count)
        raws = [[full(tiles[t][:, base + j : base + j + 1]) for t in near] for j in range(SUB)]
        for i, t in enumerate(near):
            left = solve([raws[j][i] for j in range(SUB)])
            terms = [left[j] * done[j] for j in range(SUB)]
            while len(terms) > 1:
                terms = [terms[m] + terms[m + 1] for m in range(0, len(terms), 2)]
            tiles[t] = jnp.where(inside, 0.0, tiles[t]) - terms[0]
        if far:
            top = row.astype(jnp.bfloat16).astype(jnp.float32)
            mid = (row - top).astype(jnp.bfloat16).astype(jnp.float32)
            end = row - top - mid
            left = jnp.concatenate([top, top, mid, mid, top, end], axis=0).astype(jnp.bfloat16)
            right = jnp.concatenate([top, mid, top, mid, end, top], axis=0).astype(jnp.bfloat16)
            terms = lax.dot_general(left, right, (((0,), (0,)), ((), ())), preferred_element_type=jnp.float32)
            for t in far:
                tiles[t] = jnp.where(inside, 0.0, tiles[t]) - terms[span(t, SUB), :]
    return jnp.concatenate(tiles, axis=0)


def span(i, size=LANE):
    return slice(size * i, size * (i + 1))


HALVES = (((0, 0), (1, 1), (0, 1), (0, 2), (0, 3)), ((2, 2), (3, 3), (2, 3), (1, 2), (1, 3)))
GRAM = 17
BASIS = 32


def call(kernel, outs, scalar, *args, scratch=(), near=(True,)):
    kinds = [pltpu.VMEM if here else jax.ShapeDtypeStruct for here in near]
    return pl.pallas_call(
        kernel,
        out_shape=[kind(shape, jnp.float32) for kind, shape in zip(kinds, outs)],
        in_specs=[pl.BlockSpec(memory_space=pltpu.SMEM)] + [pl.BlockSpec(memory_space=pltpu.VMEM)] * len(args),
        out_specs=[pl.BlockSpec(memory_space=pltpu.VMEM)] * len(outs),
        scratch_shapes=[pltpu.VMEM(shape, jnp.float32) for shape in scratch],
    )(scalar.reshape(1), *[pltpu.with_memory_space_constraint(a, pltpu.VMEM) for a in args])


def raw_blocks(core, mine_ref, other_ref):
    mine, other = mine_ref[...], other_ref[...]
    return jnp.where(core == 0, mine, other), jnp.where(core == 0, other, mine)


def on_diagonal():
    row = lax.broadcasted_iota(jnp.int32, (LANE, LANE), 0)
    col = lax.broadcasted_iota(jnp.int32, (LANE, LANE), 1)
    return row, col


def inner_kernel(core_ref, mine_ref, other_ref, own_ref, out_ref, *, count, pieces):
    mine, other, own = mine_ref[...], other_ref[...], own_ref[...]
    first = core_ref[0] == 0
    size, half = BASIS + GRAM, BASIS // 2
    for b, block in enumerate(raw_blocks(core_ref[0], mine_ref, other_ref)):
        gram = dot(block, own, 0, 0) / count
        for p in range(pieces // 2):
            at = size * (b * (pieces // 2) + p)
            for h in range(2):
                out_ref[at + half * h : at + half * (h + 1), :] = gram[span(p, half), span(h)]
    square = dot(mine, mine, 0, 0) / count
    left = jnp.where(first, mine[:, :LANE], other[:, LANE:])
    cross = dot(left, jnp.where(first, other, mine), 0, 0) / count
    row, col = on_diagonal()
    second = square[span(1), span(1)]
    folded = jnp.where(row <= col, square[span(0), span(0)], second)
    diagonal = jnp.sum(jnp.where(row == col, second, 0.0), axis=0, keepdims=True)
    tiles = [folded, square[span(0), span(1)], cross[:, span(0)], cross[:, span(1)]]
    each = GRAM - 1
    for p in range(pieces):
        at = size * p + BASIS
        tile, line = divmod(p * each, LANE)
        out_ref[at : at + each, :] = tiles[tile][line : line + each, :]
        out_ref[at + each : at + GRAM, :] = diagonal if p == 0 else jnp.zeros_like(diagonal)


def total_kernel(core_ref, parts_ref, tiles_ref, out_ref):
    size = BASIS + GRAM
    pieces = parts_ref.shape[0] // size
    total = parts_ref[span(0, size), :]
    for p in range(1, pieces):
        total = total + parts_ref[span(p, size), :]
    for p in range(pieces):
        tiles_ref[span(p, GRAM), :] = total[BASIS:]
    out_ref[...] = jnp.broadcast_to(total[None, :BASIS], out_ref.shape)


def unfolded(half_ref):
    each = GRAM - 1
    pieces = half_ref.shape[0] // GRAM
    rows = [half_ref[GRAM * p : GRAM * p + each, :] for p in range(pieces)]
    step = LANE // each
    folded, *rest = [jnp.concatenate(rows[step * i : step * (i + 1)], axis=0) for i in range(4)]
    diagonal = half_ref[each:GRAM, :]
    row, col = on_diagonal()
    flipped = folded.T
    first = jnp.where(row <= col, folded, flipped)
    second = jnp.where(row == col, diagonal, jnp.where(row > col, folded, flipped))
    return [first, second, *rest]


def inverse_kernel(core_ref, mine_ref, other_ref, inv_ref, work_ref):
    n = inv_ref.shape[0]
    blocks = n // LANE
    work_ref[...] = jnp.zeros_like(work_ref)
    mine, other = unfolded(mine_ref), unfolded(other_ref)
    for half in range(2):
        for at, place in enumerate(HALVES[half]):
            tile = jnp.where(core_ref[0] == half, mine[at], other[at])
            work_ref[span(place[0]), span(place[1])] = tile
    for k in range(blocks):
        done = factor(work_ref[span(k), span(k)])
        row = lax.broadcasted_iota(jnp.int32, done.shape, 0)
        col = lax.broadcasted_iota(jnp.int32, done.shape, 1)
        done = jnp.where(row >= col, done, 0.0)
        sides = [slice(0, LANE * k), slice(LANE * (k + 1), n)]
        for side in sides:
            if side.start < side.stop:
                work_ref[span(k), side] = dot(done, work_ref[span(k), side])
        work_ref[span(k), span(k)] = done
        for i in range(k + 1, blocks):
            up = work_ref[span(k), span(i)]
            work_ref[span(i), span(k)] = jnp.zeros((LANE, LANE), jnp.float32)
            for side in (slice(LANE * i, n), slice(0, LANE * (k + 1))):
                work_ref[span(i), side] = work_ref[span(i), side] - dot(up, work_ref[span(k), side], 0, 0)
    for i in range(blocks):
        split = LANE * (i + 1)
        inv_ref[span(i), :split] = work_ref[span(i), :split]
        if split < n:
            inv_ref[span(i), split:] = jnp.zeros((LANE, n - split), jnp.float32)


def basis_kernel(index_ref, mine_ref, other_ref, inv_ref, basis_ref):
    zero, one = raw_blocks(index_ref[0] % 2, mine_ref, other_ref)
    width = zero.shape[1]
    top = dot(zero, inv_ref[:width, :width], 1, 1)
    low = dot(zero, inv_ref[width:, :width], 1, 1) + dot(one, inv_ref[width:, width:], 1, 1)
    basis_ref[:, :width] = jnp.where(index_ref[0] == 1, low, top)
    basis_ref[:, width:] = low

    @pl.when(index_ref[0] > 1)
    def _():
        basis_ref[:, :width] = dot(top, inv_ref[:width, :width]) + dot(low, inv_ref[width:, :width])
        basis_ref[:, width:] = dot(low, inv_ref[width:, width:])


def finish_kernel(index_ref, basis_ref, gram_ref, own_ref, out_ref):
    width = own_ref.shape[1]
    pieces = gram_ref.shape[0]

    @pl.when(index_ref[0] < 2)
    def _():
        out_ref[...] = basis_ref[:, :width]

    @pl.when(index_ref[0] > 1)
    def _():
        for h in range(2):
            gram = gram_ref[:, span(h, BASIS // 2), :].reshape(pieces * BASIS // 2, LANE)
            out_ref[:, span(h)] = own_ref[:, span(h)] - dot(basis_ref[...], gram)


def swapped(pieces, axis):
    return lax.all_to_all(pieces, axis, 0, 0, tiled=True)


def in_lines(pieces, axis):
    lines = pieces.reshape(lax.axis_size(axis), 1, -1)
    return swapped(lines, axis).reshape(pieces.shape)


def steps(moves):
    return [(2 * source + c, 2 * target + c) for source, target in moves for c in range(2)]


def on_device(own):
    rows, width = own.shape
    many, groups = lax.axis_size("row"), lax.axis_size("orb")
    count = rows * many
    index = lax.axis_index("orb")
    core, chip = index % 2, index // 2
    pairs = [(i, i ^ 1) for i in range(groups)]

    first = lax.ppermute(own, "orb", steps([(0, 3)])) + lax.ppermute(own, "orb", steps([(0, 5)]))
    first = jnp.where(chip == 0, own, first)
    mine = first + lax.ppermute(first, "orb", steps([(0, 1), (3, 4), (5, 6)]))
    mine = mine + lax.ppermute(first, "orb", steps([(0, 7), (3, 2)]))
    other = lax.ppermute(mine, "orb", pairs)

    inner = call(
        functools.partial(inner_kernel, count=count, pieces=many),
        [(many * (BASIS + GRAM), LANE)], core, mine, other, own,
    )[0]
    tiles, gram = call(
        total_kernel, [(many * GRAM, LANE), (many, BASIS, LANE)], core, in_lines(inner, "row"),
        near=(True, False),
    )
    tiles, gram = lax.optimization_barrier((in_lines(tiles, "row"), gram))
    gram = swapped(gram, "row")
    others = lax.ppermute(tiles, "orb", pairs)
    inverse = call(
        inverse_kernel, [(2 * width, 2 * width)], core, tiles, others,
        scratch=[(2 * width, 2 * width)],
    )[0]
    basis = call(basis_kernel, [(rows, 2 * width)], index, mine, other, inverse)[0]
    return call(finish_kernel, [own.shape], index, basis, gram, own, near=(False,))[0]


def solution(mesh):
    return jax.shard_map(
        on_device,
        mesh=mesh,
        in_specs=(P("row", "orb"),),
        out_specs=P("row", "orb"),
        check_vma=False,
    )
```

```python
import functools

import jax
import jax.numpy as jnp
from jax import lax
from jax.experimental import pallas as pl
from jax.experimental.pallas import tpu as pltpu
from jax.sharding import PartitionSpec as P


SUB = 8
LANE = 128
EXACT = lax.Precision.HIGHEST


def dot(left, right, left_dim=1, right_dim=0):
    dims = (((left_dim,), (right_dim,)), ((), ()))
    return lax.dot_general(
        left, right, dims, precision=EXACT, preferred_element_type=jnp.float32
    )


NEAR = 3


def inner_sum(left, right):
    terms = [a * b for a, b in zip(left, right)]
    while len(terms) > 1:
        terms = [terms[i] + terms[i + 1] for i in range(0, len(terms), 2)]
    return terms[0]


def factor(block):
    shape = (SUB, LANE)
    lane = lax.broadcasted_iota(jnp.int32, shape, 1)
    sub = lax.broadcasted_iota(jnp.int32, shape, 0)
    count = LANE // SUB
    tiles = [block[SUB * t : SUB * (t + 1), :] for t in range(count)]

    def full(vector):
        return jnp.broadcast_to(vector, shape)

    def pick(vector, i):
        return jnp.take_along_axis(vector, jnp.full(shape, i, jnp.int32), axis=0)

    ahead = None
    for k in range(count):
        base = SUB * k
        inside = (lane >= base) & (lane < base + SUB)
        own = tiles[k]
        columns = ahead or [full(own[:, base + j : base + j + 1]) for j in range(SUB)]
        diag = [[pick(columns[j], i) for j in range(i + 1)] for i in range(SUB)]
        root, low = [], [[None] * SUB for _ in range(SUB)]
        for j in range(SUB):
            root.append(lax.rsqrt(diag[j][j]))
            for i in range(j + 1, SUB):
                low[i][j] = diag[i][j] * root[j]
            for i in range(j + 1, SUB):
                for m in range(j + 1, i + 1):
                    diag[i][m] = diag[i][m] - low[i][j] * low[m][j]

        def solve(vectors):
            for j in range(SUB):
                vectors[j] = vectors[j] * root[j]
                for i in range(j + 1, SUB):
                    vectors[i] = vectors[i] - low[i][j] * vectors[j]
            return vectors

        cleared = jnp.where(inside, jnp.where(lane - base == sub, 1.0, 0.0), own)
        done = solve([full(cleared[i : i + 1, :]) for i in range(SUB)])
        row = done[0]
        for i in range(1, SUB):
            row = jnp.where(sub == i, done[i], row)
        tiles[k] = row
        near = range(k + 1, min(k + 1 + NEAR, count))
        far = range(k + 1 + NEAR, count)
        raws = [[full(tiles[t][:, base + j : base + j + 1]) for t in near] for j in range(SUB)]
        ahead = [full(tiles[t][:, base + SUB + j : base + SUB + j + 1]) for t in near[:1] for j in range(SUB)]
        for i, t in enumerate(near):
            left = solve([raws[j][i] for j in range(SUB)])
            if i == 0:
                ahead = [c - inner_sum(left, [pick(v, j) for v in left]) for j, c in enumerate(ahead)]
            tiles[t] = jnp.where(inside, 0.0, tiles[t]) - inner_sum(left, done)
        if far:
            top = row.astype(jnp.bfloat16).astype(jnp.float32)
            mid = (row - top).astype(jnp.bfloat16).astype(jnp.float32)
            end = row - top - mid
            left = jnp.concatenate([top, top, mid, mid, top, end], axis=0).astype(jnp.bfloat16)
            right = jnp.concatenate([top, mid, top, mid, end, top], axis=0).astype(jnp.bfloat16)
            terms = lax.dot_general(left, right, (((0,), (0,)), ((), ())), preferred_element_type=jnp.float32)
            for t in far:
                tiles[t] = jnp.where(inside, 0.0, tiles[t]) - terms[span(t, SUB), :]
    return jnp.concatenate(tiles, axis=0)


def span(i, size=LANE):
    return slice(size * i, size * (i + 1))


HALVES = (((0, 0), (1, 1), (0, 1), (0, 2), (0, 3)), ((2, 2), (3, 3), (2, 3), (1, 2), (1, 3)))
GRAM = 17
BASIS = 32


def call(kernel, outs, scalar, *args, scratch=(), near=(True,)):
    kinds = [pltpu.VMEM if here else jax.ShapeDtypeStruct for here in near]
    return pl.pallas_call(
        kernel,
        out_shape=[kind(shape, jnp.float32) for kind, shape in zip(kinds, outs)],
        in_specs=[pl.BlockSpec(memory_space=pltpu.SMEM)] + [pl.BlockSpec(memory_space=pltpu.VMEM)] * len(args),
        out_specs=[pl.BlockSpec(memory_space=pltpu.VMEM)] * len(outs),
        scratch_shapes=[pltpu.VMEM(shape, jnp.float32) for shape in scratch],
    )(scalar.reshape(1), *[pltpu.with_memory_space_constraint(a, pltpu.VMEM) for a in args])


def raw_blocks(core, mine_ref, other_ref):
    mine, other = mine_ref[...], other_ref[...]
    return jnp.where(core == 0, mine, other), jnp.where(core == 0, other, mine)


def on_diagonal():
    row = lax.broadcasted_iota(jnp.int32, (LANE, LANE), 0)
    col = lax.broadcasted_iota(jnp.int32, (LANE, LANE), 1)
    return row, col


def inner_kernel(core_ref, mine_ref, other_ref, own_ref, out_ref, *, count, pieces):
    mine, other, own = mine_ref[...], other_ref[...], own_ref[...]
    first = core_ref[0] == 0
    size, half = BASIS + GRAM, BASIS // 2
    for b, block in enumerate(raw_blocks(core_ref[0], mine_ref, other_ref)):
        gram = dot(block, own, 0, 0) / count
        for p in range(pieces // 2):
            at = size * (b * (pieces // 2) + p)
            for h in range(2):
                out_ref[at + half * h : at + half * (h + 1), :] = gram[span(p, half), span(h)]
    square = dot(mine, mine, 0, 0) / count
    left = jnp.where(first, mine[:, :LANE], other[:, LANE:])
    cross = dot(left, jnp.where(first, other, mine), 0, 0) / count
    row, col = on_diagonal()
    second = square[span(1), span(1)]
    folded = jnp.where(row <= col, square[span(0), span(0)], second)
    diagonal = jnp.sum(jnp.where(row == col, second, 0.0), axis=0, keepdims=True)
    tiles = [folded, square[span(0), span(1)], cross[:, span(0)], cross[:, span(1)]]
    each = GRAM - 1
    for p in range(pieces):
        at = size * p + BASIS
        tile, line = divmod(p * each, LANE)
        out_ref[at : at + each, :] = tiles[tile][line : line + each, :]
        out_ref[at + each : at + GRAM, :] = diagonal if p == 0 else jnp.zeros_like(diagonal)


def total_kernel(core_ref, parts_ref, tiles_ref, out_ref):
    size = BASIS + GRAM
    pieces = parts_ref.shape[0] // size
    total = parts_ref[span(0, size), :]
    for p in range(1, pieces):
        total = total + parts_ref[span(p, size), :]
    for p in range(pieces):
        tiles_ref[span(p, GRAM), :] = total[BASIS:]
    out_ref[...] = jnp.broadcast_to(total[None, :BASIS], out_ref.shape)


def unfolded(half_ref):
    each = GRAM - 1
    pieces = half_ref.shape[0] // GRAM
    rows = [half_ref[GRAM * p : GRAM * p + each, :] for p in range(pieces)]
    step = LANE // each
    folded, *rest = [jnp.concatenate(rows[step * i : step * (i + 1)], axis=0) for i in range(4)]
    diagonal = half_ref[each:GRAM, :]
    row, col = on_diagonal()
    flipped = folded.T
    first = jnp.where(row <= col, folded, flipped)
    second = jnp.where(row == col, diagonal, jnp.where(row > col, folded, flipped))
    return [first, second, *rest]


def inverse_kernel(core_ref, mine_ref, other_ref, inv_ref, work_ref):
    n = inv_ref.shape[0]
    blocks = n // LANE
    work_ref[...] = jnp.zeros_like(work_ref)
    mine, other = unfolded(mine_ref), unfolded(other_ref)
    for half in range(2):
        for at, place in enumerate(HALVES[half]):
            tile = jnp.where(core_ref[0] == half, mine[at], other[at])
            work_ref[span(place[0]), span(place[1])] = tile
    for k in range(blocks):
        done = factor(work_ref[span(k), span(k)])
        row, col = on_diagonal()
        done = jnp.where(row >= col, done, 0.0)
        if k + 1 < blocks:
            up = dot(done, work_ref[span(k), span(k + 1)])
            work_ref[span(k + 1), span(k + 1)] = work_ref[span(k + 1), span(k + 1)] - dot(up, up, 0, 0)
        for j in range(blocks):
            if j != k:
                work_ref[span(k), span(j)] = up if j == k + 1 else dot(done, work_ref[span(k), span(j)])
        work_ref[span(k), span(k)] = done
        for i in range(k + 1, blocks):
            up = work_ref[span(k), span(i)]
            work_ref[span(i), span(k)] = jnp.zeros((LANE, LANE), jnp.float32)
            for j in [*range(i, blocks), *range(k + 1)]:
                if (i, j) != (k + 1, k + 1):
                    change = dot(up, work_ref[span(k), span(j)], 0, 0)
                    work_ref[span(i), span(j)] = work_ref[span(i), span(j)] - change
    for i in range(blocks):
        split = LANE * (i + 1)
        inv_ref[span(i), :split] = work_ref[span(i), :split]
        if split < n:
            inv_ref[span(i), split:] = jnp.zeros((LANE, n - split), jnp.float32)


def basis_kernel(index_ref, mine_ref, other_ref, inv_ref, basis_ref):
    zero, one = raw_blocks(index_ref[0] % 2, mine_ref, other_ref)
    width = zero.shape[1]
    top = dot(zero, inv_ref[:width, :width], 1, 1)
    low = dot(zero, inv_ref[width:, :width], 1, 1) + dot(one, inv_ref[width:, width:], 1, 1)
    basis_ref[:, :width] = jnp.where(index_ref[0] == 1, low, top)
    basis_ref[:, width:] = low

    @pl.when(index_ref[0] > 1)
    def _():
        basis_ref[:, :width] = dot(top, inv_ref[:width, :width]) + dot(low, inv_ref[width:, :width])
        basis_ref[:, width:] = dot(low, inv_ref[width:, width:])


def finish_kernel(index_ref, basis_ref, gram_ref, own_ref, out_ref):
    width = own_ref.shape[1]
    pieces = gram_ref.shape[0]

    @pl.when(index_ref[0] < 2)
    def _():
        out_ref[...] = basis_ref[:, :width]

    @pl.when(index_ref[0] > 1)
    def _():
        for h in range(2):
            gram = gram_ref[:, span(h, BASIS // 2), :].reshape(pieces * BASIS // 2, LANE)
            out_ref[:, span(h)] = own_ref[:, span(h)] - dot(basis_ref[...], gram)


def swapped(pieces, axis):
    return lax.all_to_all(pieces, axis, 0, 0, tiled=True)


def in_lines(pieces, axis):
    lines = pieces.reshape(lax.axis_size(axis), 1, -1)
    return swapped(lines, axis).reshape(pieces.shape)


def steps(moves):
    return [(2 * source + c, 2 * target + c) for source, target in moves for c in range(2)]


def on_device(own):
    rows, width = own.shape
    many, groups = lax.axis_size("row"), lax.axis_size("orb")
    count = rows * many
    index = lax.axis_index("orb")
    core, chip = index % 2, index // 2
    pairs = [(i, i ^ 1) for i in range(groups)]

    first = lax.ppermute(own, "orb", steps([(0, 3)])) + lax.ppermute(own, "orb", steps([(0, 5)]))
    first = jnp.where(chip == 0, own, first)
    mine = first + lax.ppermute(first, "orb", steps([(0, 1), (3, 4), (5, 6)]))
    mine = mine + lax.ppermute(first, "orb", steps([(0, 7), (3, 2)]))
    other = lax.ppermute(mine, "orb", pairs)

    inner = call(
        functools.partial(inner_kernel, count=count, pieces=many),
        [(many * (BASIS + GRAM), LANE)], core, mine, other, own,
    )[0]
    tiles, gram = call(
        total_kernel, [(many * GRAM, LANE), (many, BASIS, LANE)], core, in_lines(inner, "row"),
        near=(True, False),
    )
    tiles, gram = lax.optimization_barrier((in_lines(tiles, "row"), gram))
    gram = swapped(gram, "row")
    others = lax.ppermute(tiles, "orb", pairs)
    inverse = call(
        inverse_kernel, [(2 * width, 2 * width)], core, tiles, others,
        scratch=[(2 * width, 2 * width)],
    )[0]
    basis = call(basis_kernel, [(rows, 2 * width)], index, mine, other, inverse)[0]
    return call(finish_kernel, [own.shape], index, basis, gram, own, near=(False,))[0]


def solution(mesh):
    return jax.shard_map(
        on_device,
        mesh=mesh,
        in_specs=(P("row", "orb"),),
        out_specs=P("row", "orb"),
        check_vma=False,
    )
```

```python
import functools

import jax
import jax.numpy as jnp
from jax import lax
from jax.experimental import pallas as pl
from jax.experimental.pallas import tpu as pltpu
from jax.sharding import PartitionSpec as P


SUB = 8
LANE = 128
EXACT = lax.Precision.HIGHEST


def dot(left, right, left_dim=1, right_dim=0):
    dims = (((left_dim,), (right_dim,)), ((), ()))
    return lax.dot_general(
        left, right, dims, precision=EXACT, preferred_element_type=jnp.float32
    )


NEAR = 3


def inner_sum(left, right):
    terms = [a * b for a, b in zip(left, right)]
    while len(terms) > 1:
        terms = [terms[i] + terms[i + 1] for i in range(0, len(terms), 2)]
    return terms[0]


def factor(block):
    shape = (SUB, LANE)
    lane = lax.broadcasted_iota(jnp.int32, shape, 1)
    sub = lax.broadcasted_iota(jnp.int32, shape, 0)
    count = LANE // SUB
    tiles = [block[SUB * t : SUB * (t + 1), :] for t in range(count)]

    def full(vector):
        return jnp.broadcast_to(vector, shape)

    def pick(vector, i):
        return jnp.take_along_axis(vector, jnp.full(shape, i, jnp.int32), axis=0)

    ahead = None
    for k in range(count):
        base = SUB * k
        inside = (lane >= base) & (lane < base + SUB)
        own = tiles[k]
        columns = ahead or [full(own[:, base + j : base + j + 1]) for j in range(SUB)]
        diag = [[pick(columns[j], i) for j in range(i + 1)] for i in range(SUB)]
        root, low = [], [[None] * SUB for _ in range(SUB)]
        for j in range(SUB):
            root.append(lax.rsqrt(diag[j][j]))
            for i in range(j + 1, SUB):
                low[i][j] = diag[i][j] * root[j]
            for i in range(j + 1, SUB):
                for m in range(j + 1, i + 1):
                    diag[i][m] = diag[i][m] - low[i][j] * low[m][j]

        def solve(vectors):
            for j in range(SUB):
                vectors[j] = vectors[j] * root[j]
                for i in range(j + 1, SUB):
                    vectors[i] = vectors[i] - low[i][j] * vectors[j]
            return vectors

        cleared = jnp.where(inside, jnp.where(lane - base == sub, 1.0, 0.0), own)
        done = solve([full(cleared[i : i + 1, :]) for i in range(SUB)])
        row = done[0]
        for i in range(1, SUB):
            row = jnp.where(sub == i, done[i], row)
        tiles[k] = row
        near = range(k + 1, min(k + 1 + NEAR, count))
        far = range(k + 1 + NEAR, count)
        raws = [[full(tiles[t][:, base + j : base + j + 1]) for t in near] for j in range(SUB)]
        ahead = [full(tiles[t][:, base + SUB + j : base + SUB + j + 1]) for t in near[:1] for j in range(SUB)]
        for i, t in enumerate(near):
            left = solve([raws[j][i] for j in range(SUB)])
            if i == 0:
                ahead = [c - inner_sum(left, [pick(v, j) for v in left]) for j, c in enumerate(ahead)]
            tiles[t] = jnp.where(inside, 0.0, tiles[t]) - inner_sum(left, done)
        if far:
            top = row.astype(jnp.bfloat16).astype(jnp.float32)
            mid = (row - top).astype(jnp.bfloat16).astype(jnp.float32)
            end = row - top - mid
            left = jnp.concatenate([top, top, mid, mid, top, end], axis=0).astype(jnp.bfloat16)
            right = jnp.concatenate([top, mid, top, mid, end, top], axis=0).astype(jnp.bfloat16)
            terms = lax.dot_general(left, right, (((0,), (0,)), ((), ())), preferred_element_type=jnp.float32)
            for t in far:
                tiles[t] = jnp.where(inside, 0.0, tiles[t]) - terms[span(t, SUB), :]
    return jnp.concatenate(tiles, axis=0)


def span(i, size=LANE):
    return slice(size * i, size * (i + 1))


HALVES = (((0, 0), (1, 1), (0, 1), (0, 2), (0, 3)), ((2, 2), (3, 3), (2, 3), (1, 2), (1, 3)))
GRAM = 17
BASIS = 32


def call(kernel, outs, scalar, *args, scratch=(), near=(True,)):
    kinds = [pltpu.VMEM if here else jax.ShapeDtypeStruct for here in near]
    return pl.pallas_call(
        kernel,
        out_shape=[kind(shape, jnp.float32) for kind, shape in zip(kinds, outs)],
        in_specs=[pl.BlockSpec(memory_space=pltpu.SMEM)] + [pl.BlockSpec(memory_space=pltpu.VMEM)] * len(args),
        out_specs=[pl.BlockSpec(memory_space=pltpu.VMEM)] * len(outs),
        scratch_shapes=[pltpu.VMEM(shape, jnp.float32) for shape in scratch],
    )(scalar.reshape(1), *[pltpu.with_memory_space_constraint(a, pltpu.VMEM) for a in args])


def raw_blocks(core, mine_ref, other_ref):
    mine, other = mine_ref[...], other_ref[...]
    return jnp.where(core == 0, mine, other), jnp.where(core == 0, other, mine)


def on_diagonal():
    row = lax.broadcasted_iota(jnp.int32, (LANE, LANE), 0)
    col = lax.broadcasted_iota(jnp.int32, (LANE, LANE), 1)
    return row, col


def inner_kernel(core_ref, mine_ref, other_ref, own_ref, out_ref, *, count, pieces):
    mine, other, own = mine_ref[...], other_ref[...], own_ref[...]
    first = core_ref[0] == 0
    size, half = BASIS + GRAM, BASIS // 2
    for b, block in enumerate(raw_blocks(core_ref[0], mine_ref, other_ref)):
        gram = dot(block, own, 0, 0) / count
        for p in range(pieces // 2):
            at = size * (b * (pieces // 2) + p)
            for h in range(2):
                out_ref[at + half * h : at + half * (h + 1), :] = gram[span(p, half), span(h)]
    square = dot(mine, mine, 0, 0) / count
    left = jnp.where(first, mine[:, :LANE], other[:, LANE:])
    cross = dot(left, jnp.where(first, other, mine), 0, 0) / count
    row, col = on_diagonal()
    second = square[span(1), span(1)]
    folded = jnp.where(row <= col, square[span(0), span(0)], second)
    diagonal = jnp.sum(jnp.where(row == col, second, 0.0), axis=0, keepdims=True)
    tiles = [folded, square[span(0), span(1)], cross[:, span(0)], cross[:, span(1)]]
    each = GRAM - 1
    for p in range(pieces):
        at = size * p + BASIS
        tile, line = divmod(p * each, LANE)
        out_ref[at : at + each, :] = tiles[tile][line : line + each, :]
        out_ref[at + each : at + GRAM, :] = diagonal if p == 0 else jnp.zeros_like(diagonal)


def total_kernel(core_ref, parts_ref, tiles_ref, out_ref):
    size = BASIS + GRAM
    pieces = parts_ref.shape[0] // size
    total = parts_ref[span(0, size), :]
    for p in range(1, pieces):
        total = total + parts_ref[span(p, size), :]
    for p in range(pieces):
        tiles_ref[span(p, GRAM), :] = total[BASIS:]
    out_ref[...] = jnp.broadcast_to(total[None, :BASIS], out_ref.shape)


def unfolded(half_ref):
    each = GRAM - 1
    pieces = half_ref.shape[0] // GRAM
    rows = [half_ref[GRAM * p : GRAM * p + each, :] for p in range(pieces)]
    step = LANE // each
    folded, *rest = [jnp.concatenate(rows[step * i : step * (i + 1)], axis=0) for i in range(4)]
    diagonal = half_ref[each:GRAM, :]
    row, col = on_diagonal()
    flipped = folded.T
    first = jnp.where(row <= col, folded, flipped)
    second = jnp.where(row == col, diagonal, jnp.where(row > col, folded, flipped))
    return [first, second, *rest]


def basis_kernel(index_ref, near_ref, far_ref, mine_ref, other_ref, basis_ref, work_ref, raw_ref, q_ref):
    n, width = work_ref.shape[0], near_ref.shape[1]
    blocks = n // LANE
    core = index_ref[0] % 2
    raw_ref[:, :width], raw_ref[:, width:] = raw_blocks(core, near_ref, far_ref)
    basis_ref[...] = jnp.zeros_like(basis_ref)
    work_ref[...] = jnp.zeros_like(work_ref)
    mine, other = unfolded(mine_ref), unfolded(other_ref)
    for half in range(2):
        for at, place in enumerate(HALVES[half]):
            tile = jnp.where(core == half, mine[at], other[at])
            work_ref[span(place[0]), span(place[1])] = tile
    for k in range(blocks):
        done = factor(work_ref[span(k), span(k)])
        row, col = on_diagonal()
        done = jnp.where(row >= col, done, 0.0)
        if k + 1 < blocks:
            up = dot(done, work_ref[span(k), span(k + 1)])
            work_ref[span(k + 1), span(k + 1)] = work_ref[span(k + 1), span(k + 1)] - dot(up, up, 0, 0)
        for j in range(blocks):
            if j != k:
                work_ref[span(k), span(j)] = up if j == k + 1 else dot(done, work_ref[span(k), span(j)])
        work_ref[span(k), span(k)] = done
        for i in range(k + 1, blocks):
            up = work_ref[span(k), span(i)]
            work_ref[span(i), span(k)] = jnp.zeros((LANE, LANE), jnp.float32)
            for j in [*range(i, blocks), *range(k + 1)]:
                if (i, j) != (k + 1, k + 1):
                    change = dot(up, work_ref[span(k), span(j)], 0, 0)
                    work_ref[span(i), span(j)] = work_ref[span(i), span(j)] - change
        known = slice(0, LANE * (k + 1))
        part = dot(raw_ref[:, known], work_ref[span(k), known], 1, 1)
        q_ref[:, span(k)] = part
        basis_ref[:, known] = basis_ref[:, known] + dot(part, work_ref[span(k), known])

    @pl.when(index_ref[0] < 2)
    def _():
        basis_ref[:, :width] = jnp.where(core == 0, q_ref[:, :width], q_ref[:, width:])


def finish_kernel(index_ref, basis_ref, gram_ref, own_ref, out_ref):
    width = own_ref.shape[1]
    pieces = gram_ref.shape[0]

    @pl.when(index_ref[0] < 2)
    def _():
        out_ref[...] = basis_ref[:, :width]

    @pl.when(index_ref[0] > 1)
    def _():
        for h in range(2):
            gram = gram_ref[:, span(h, BASIS // 2), :].reshape(pieces * BASIS // 2, LANE)
            out_ref[:, span(h)] = own_ref[:, span(h)] - dot(basis_ref[...], gram)


def swapped(pieces, axis):
    return lax.all_to_all(pieces, axis, 0, 0, tiled=True)


def in_lines(pieces, axis):
    lines = pieces.reshape(lax.axis_size(axis), 1, -1)
    return swapped(lines, axis).reshape(pieces.shape)


def steps(moves):
    return [(2 * source + c, 2 * target + c) for source, target in moves for c in range(2)]


def on_device(own):
    rows, width = own.shape
    many, groups = lax.axis_size("row"), lax.axis_size("orb")
    count = rows * many
    index = lax.axis_index("orb")
    core, chip = index % 2, index // 2
    pairs = [(i, i ^ 1) for i in range(groups)]

    given = [lax.ppermute(own, "orb", steps([(0, target)])) for target in (5, 3, 7, 1)]
    first = jnp.where(chip == 0, own, (given[0] + given[1]) + (given[2] + given[3]))
    mine = first + lax.ppermute(first, "orb", steps([(1, 2), (3, 4), (5, 6)]))
    other = lax.ppermute(mine, "orb", pairs)

    inner = call(
        functools.partial(inner_kernel, count=count, pieces=many),
        [(many * (BASIS + GRAM), LANE)], core, mine, other, own,
    )[0]
    tiles, gram = call(
        total_kernel, [(many * GRAM, LANE), (many, BASIS, LANE)], core, in_lines(inner, "row"),
        near=(True, False),
    )
    tiles, gram = lax.optimization_barrier((in_lines(tiles, "row"), gram))
    gram = swapped(gram, "row")
    others = lax.ppermute(tiles, "orb", pairs)
    basis = call(
        basis_kernel, [(rows, 2 * width)], index, mine, other, tiles, others,
        scratch=[(2 * width, 2 * width)] + [(rows, 2 * width)] * 2,
    )[0]
    return call(finish_kernel, [own.shape], index, basis, gram, own, near=(False,))[0]


def solution(mesh):
    return jax.shard_map(
        on_device,
        mesh=mesh,
        in_specs=(P("row", "orb"),),
        out_specs=P("row", "orb"),
        check_vma=False,
    )
```

```python
import functools

import jax
import jax.numpy as jnp
from jax import lax
from jax.experimental import pallas as pl
from jax.experimental.pallas import tpu as pltpu
from jax.sharding import PartitionSpec as P


SUB = 8
LANE = 128
EXACT = lax.Precision.HIGHEST


def dot(left, right, left_dim=1, right_dim=0):
    dims = (((left_dim,), (right_dim,)), ((), ()))
    return lax.dot_general(
        left, right, dims, precision=EXACT, preferred_element_type=jnp.float32
    )


NEAR = 3


def inner_sum(left, right):
    terms = [a * b for a, b in zip(left, right)]
    while len(terms) > 1:
        terms = [terms[i] + terms[i + 1] for i in range(0, len(terms), 2)]
    return terms[0]


def factor(block):
    shape = (SUB, LANE)
    lane = lax.broadcasted_iota(jnp.int32, shape, 1)
    sub = lax.broadcasted_iota(jnp.int32, shape, 0)
    count = LANE // SUB
    tiles = [block[SUB * t : SUB * (t + 1), :] for t in range(count)]

    def full(vector):
        return jnp.broadcast_to(vector, shape)

    def pick(vector, i):
        return jnp.take_along_axis(vector, jnp.full(shape, i, jnp.int32), axis=0)

    ahead = None
    for k in range(count):
        base = SUB * k
        inside = (lane >= base) & (lane < base + SUB)
        own = tiles[k]
        columns = ahead or [full(own[:, base + j : base + j + 1]) for j in range(SUB)]
        diag = [[pick(columns[j], i) for j in range(i + 1)] for i in range(SUB)]
        root, low = [], [[None] * SUB for _ in range(SUB)]
        for j in range(SUB):
            root.append(lax.rsqrt(diag[j][j]))
            for i in range(j + 1, SUB):
                low[i][j] = diag[i][j] * root[j]
            for i in range(j + 1, SUB):
                for m in range(j + 1, i + 1):
                    diag[i][m] = diag[i][m] - low[i][j] * low[m][j]

        def solve(vectors):
            for j in range(SUB):
                vectors[j] = vectors[j] * root[j]
                for i in range(j + 1, SUB):
                    vectors[i] = vectors[i] - low[i][j] * vectors[j]
            return vectors

        cleared = jnp.where(inside, jnp.where(lane - base == sub, 1.0, 0.0), own)
        done = solve([full(cleared[i : i + 1, :]) for i in range(SUB)])
        row = done[0]
        for i in range(1, SUB):
            row = jnp.where(sub == i, done[i], row)
        tiles[k] = row
        near = range(k + 1, min(k + 1 + NEAR, count))
        far = range(k + 1 + NEAR, count)
        raws = [[full(tiles[t][:, base + j : base + j + 1]) for t in near] for j in range(SUB)]
        ahead = [full(tiles[t][:, base + SUB + j : base + SUB + j + 1]) for t in near[:1] for j in range(SUB)]
        for i, t in enumerate(near):
            left = solve([raws[j][i] for j in range(SUB)])
            if i == 0:
                ahead = [c - inner_sum(left, [pick(v, j) for v in left]) for j, c in enumerate(ahead)]
            tiles[t] = jnp.where(inside, 0.0, tiles[t]) - inner_sum(left, done)
        if far:
            top = row.astype(jnp.bfloat16).astype(jnp.float32)
            mid = (row - top).astype(jnp.bfloat16).astype(jnp.float32)
            end = row - top - mid
            left = jnp.concatenate([top, top, mid, mid, top, end], axis=0).astype(jnp.bfloat16)
            right = jnp.concatenate([top, mid, top, mid, end, top], axis=0).astype(jnp.bfloat16)
            terms = lax.dot_general(left, right, (((0,), (0,)), ((), ())), preferred_element_type=jnp.float32)
            for t in far:
                tiles[t] = jnp.where(inside, 0.0, tiles[t]) - terms[span(t, SUB), :]
    return jnp.concatenate(tiles, axis=0)


def span(i, size=LANE):
    return slice(size * i, size * (i + 1))


HALVES = (((0, 0), (1, 1), (0, 1), (0, 2), (0, 3)), ((2, 2), (3, 3), (2, 3), (1, 2), (1, 3)))
GRAM = 17
BASIS = 32


def call(kernel, outs, scalar, *args, scratch=(), near=(True,)):
    kinds = [pltpu.VMEM if here else jax.ShapeDtypeStruct for here in near]
    return pl.pallas_call(
        kernel,
        out_shape=[kind(shape, jnp.float32) for kind, shape in zip(kinds, outs)],
        in_specs=[pl.BlockSpec(memory_space=pltpu.SMEM)] + [pl.BlockSpec(memory_space=pltpu.VMEM)] * len(args),
        out_specs=[pl.BlockSpec(memory_space=pltpu.VMEM)] * len(outs),
        scratch_shapes=[pltpu.VMEM(shape, jnp.float32) for shape in scratch],
    )(scalar.reshape(1), *[pltpu.with_memory_space_constraint(a, pltpu.VMEM) for a in args])


def raw_blocks(core, mine_ref, other_ref):
    mine, other = mine_ref[...], other_ref[...]
    return jnp.where(core == 0, mine, other), jnp.where(core == 0, other, mine)


def on_diagonal():
    row = lax.broadcasted_iota(jnp.int32, (LANE, LANE), 0)
    col = lax.broadcasted_iota(jnp.int32, (LANE, LANE), 1)
    return row, col


def inner_kernel(core_ref, mine_ref, other_ref, own_ref, out_ref, *, count, pieces):
    mine, other, own = mine_ref[...], other_ref[...], own_ref[...]
    first = core_ref[0] == 0
    size, half = BASIS + GRAM, BASIS // 2
    for b, block in enumerate(raw_blocks(core_ref[0], mine_ref, other_ref)):
        gram = dot(block, own, 0, 0) / count
        for p in range(pieces // 2):
            at = size * (b * (pieces // 2) + p)
            for h in range(2):
                out_ref[at + half * h : at + half * (h + 1), :] = gram[span(p, half), span(h)]
    square = dot(mine, mine, 0, 0) / count
    left = jnp.where(first, mine[:, :LANE], other[:, LANE:])
    cross = dot(left, jnp.where(first, other, mine), 0, 0) / count
    row, col = on_diagonal()
    second = square[span(1), span(1)]
    folded = jnp.where(row <= col, square[span(0), span(0)], second)
    diagonal = jnp.sum(jnp.where(row == col, second, 0.0), axis=0, keepdims=True)
    tiles = [folded, square[span(0), span(1)], cross[:, span(0)], cross[:, span(1)]]
    each = GRAM - 1
    for p in range(pieces):
        at = size * p + BASIS
        tile, line = divmod(p * each, LANE)
        out_ref[at : at + each, :] = tiles[tile][line : line + each, :]
        out_ref[at + each : at + GRAM, :] = diagonal if p == 0 else jnp.zeros_like(diagonal)


def total_kernel(core_ref, parts_ref, tiles_ref, out_ref):
    size = BASIS + GRAM
    pieces = parts_ref.shape[0] // size
    total = parts_ref[span(0, size), :]
    for p in range(1, pieces):
        total = total + parts_ref[span(p, size), :]
    for p in range(pieces):
        tiles_ref[span(p, GRAM), :] = total[BASIS:]
    out_ref[...] = jnp.broadcast_to(total[None, :BASIS], out_ref.shape)


def unfolded(half_ref):
    each = GRAM - 1
    pieces = half_ref.shape[0] // GRAM
    rows = [half_ref[GRAM * p : GRAM * p + each, :] for p in range(pieces)]
    step = LANE // each
    folded, *rest = [jnp.concatenate(rows[step * i : step * (i + 1)], axis=0) for i in range(4)]
    diagonal = half_ref[each:GRAM, :]
    row, col = on_diagonal()
    flipped = folded.T
    first = jnp.where(row <= col, folded, flipped)
    second = jnp.where(row == col, diagonal, jnp.where(row > col, folded, flipped))
    return [first, second, *rest]


def inverse_kernel(core_ref, mine_ref, other_ref, inv_ref, work_ref):
    n = inv_ref.shape[0]
    blocks = n // LANE
    work_ref[...] = jnp.zeros_like(work_ref)
    mine, other = unfolded(mine_ref), unfolded(other_ref)
    for half in range(2):
        for at, place in enumerate(HALVES[half]):
            tile = jnp.where(core_ref[0] == half, mine[at], other[at])
            work_ref[span(place[0]), span(place[1])] = tile
    for k in range(blocks):
        done = factor(work_ref[span(k), span(k)])
        row, col = on_diagonal()
        done = jnp.where(row >= col, done, 0.0)
        if k + 1 < blocks:
            up = dot(done, work_ref[span(k), span(k + 1)])
            work_ref[span(k + 1), span(k + 1)] = work_ref[span(k + 1), span(k + 1)] - dot(up, up, 0, 0)
        for j in range(blocks):
            if j != k:
                work_ref[span(k), span(j)] = up if j == k + 1 else dot(done, work_ref[span(k), span(j)])
        work_ref[span(k), span(k)] = done
        for i in range(k + 1, blocks):
            up = work_ref[span(k), span(i)]
            work_ref[span(i), span(k)] = jnp.zeros((LANE, LANE), jnp.float32)
            for j in [*range(i, blocks), *range(k + 1)]:
                if (i, j) != (k + 1, k + 1):
                    change = dot(up, work_ref[span(k), span(j)], 0, 0)
                    work_ref[span(i), span(j)] = work_ref[span(i), span(j)] - change
    for i in range(blocks):
        split = LANE * (i + 1)
        inv_ref[span(i), :split] = work_ref[span(i), :split]
        if split < n:
            inv_ref[span(i), split:] = jnp.zeros((LANE, n - split), jnp.float32)


def basis_kernel(index_ref, mine_ref, other_ref, inv_ref, basis_ref):
    zero, one = raw_blocks(index_ref[0] % 2, mine_ref, other_ref)
    width = zero.shape[1]
    top = dot(zero, inv_ref[:width, :width], 1, 1)
    low = dot(zero, inv_ref[width:, :width], 1, 1) + dot(one, inv_ref[width:, width:], 1, 1)
    basis_ref[:, :width] = jnp.where(index_ref[0] == 1, low, top)
    basis_ref[:, width:] = low

    @pl.when(index_ref[0] > 1)
    def _():
        basis_ref[:, :width] = dot(top, inv_ref[:width, :width]) + dot(low, inv_ref[width:, :width])
        basis_ref[:, width:] = dot(low, inv_ref[width:, width:])


def finish_kernel(index_ref, basis_ref, gram_ref, own_ref, out_ref):
    width = own_ref.shape[1]
    pieces = gram_ref.shape[0]

    @pl.when(index_ref[0] < 2)
    def _():
        out_ref[...] = basis_ref[:, :width]

    @pl.when(index_ref[0] > 1)
    def _():
        for h in range(2):
            gram = gram_ref[:, span(h, BASIS // 2), :].reshape(pieces * BASIS // 2, LANE)
            out_ref[:, span(h)] = own_ref[:, span(h)] - dot(basis_ref[...], gram)


def swapped(pieces, axis):
    return lax.all_to_all(pieces, axis, 0, 0, tiled=True)


def in_lines(pieces, axis):
    lines = pieces.reshape(lax.axis_size(axis), 1, -1)
    return swapped(lines, axis).reshape(pieces.shape)


def steps(moves):
    return [(2 * source + c, 2 * target + c) for source, target in moves for c in range(2)]


def on_device(own):
    rows, width = own.shape
    many, groups = lax.axis_size("row"), lax.axis_size("orb")
    count = rows * many
    index = lax.axis_index("orb")
    core, chip = index % 2, index // 2
    pairs = [(i, i ^ 1) for i in range(groups)]

    given = [lax.ppermute(own, "orb", steps([(0, target)])) for target in (5, 7, 3, 1)]
    first = jnp.where(chip == 0, own, (given[0] + given[1]) + (given[2] + given[3]))
    mine = first + lax.ppermute(first, "orb", steps([(1, 2), (3, 4), (7, 6)]))
    other = lax.ppermute(mine, "orb", pairs)

    inner = call(
        functools.partial(inner_kernel, count=count, pieces=many),
        [(many * (BASIS + GRAM), LANE)], core, mine, other, own,
    )[0]
    tiles, gram = call(
        total_kernel, [(many * GRAM, LANE), (many, BASIS, LANE)], core, in_lines(inner, "row"),
        near=(True, False),
    )
    tiles, gram = lax.optimization_barrier((in_lines(tiles, "row"), gram))
    gram = swapped(gram, "row")
    others = lax.ppermute(tiles, "orb", pairs)
    inverse = call(
        inverse_kernel, [(2 * width, 2 * width)], core, tiles, others,
        scratch=[(2 * width, 2 * width)],
    )[0]
    basis = call(basis_kernel, [(rows, 2 * width)], index, mine, other, inverse)[0]
    return call(finish_kernel, [own.shape], index, basis, gram, own, near=(False,))[0]


def solution(mesh):
    return jax.shard_map(
        on_device,
        mesh=mesh,
        in_specs=(P("row", "orb"),),
        out_specs=P("row", "orb"),
        check_vma=False,
    )
```

```python
import functools

import jax
import jax.numpy as jnp
from jax import lax
from jax.experimental import pallas as pl
from jax.experimental.pallas import tpu as pltpu
from jax.sharding import PartitionSpec as P


SUB = 8
LANE = 128
EXACT = lax.Precision.HIGHEST


def dot(left, right, left_dim=1, right_dim=0):
    dims = (((left_dim,), (right_dim,)), ((), ()))
    return lax.dot_general(
        left, right, dims, precision=EXACT, preferred_element_type=jnp.float32
    )


NEAR = 3


def inner_sum(left, right):
    terms = [a * b for a, b in zip(left, right)]
    while len(terms) > 1:
        terms = [terms[i] + terms[i + 1] for i in range(0, len(terms), 2)]
    return terms[0]


def factor(block):
    shape = (SUB, LANE)
    lane = lax.broadcasted_iota(jnp.int32, shape, 1)
    sub = lax.broadcasted_iota(jnp.int32, shape, 0)
    count = LANE // SUB
    tiles = [block[SUB * t : SUB * (t + 1), :] for t in range(count)]

    def full(vector):
        return jnp.broadcast_to(vector, shape)

    def pick(vector, i):
        return jnp.take_along_axis(vector, jnp.full(shape, i, jnp.int32), axis=0)

    ahead = None
    for k in range(count):
        base = SUB * k
        inside = (lane >= base) & (lane < base + SUB)
        own = tiles[k]
        columns = ahead or [full(own[:, base + j : base + j + 1]) for j in range(SUB)]
        diag = [[pick(columns[j], i) for j in range(i + 1)] for i in range(SUB)]
        root, low = [], [[None] * SUB for _ in range(SUB)]
        for j in range(SUB):
            root.append(lax.rsqrt(diag[j][j]))
            for i in range(j + 1, SUB):
                low[i][j] = diag[i][j] * root[j]
            for i in range(j + 1, SUB):
                for m in range(j + 1, i + 1):
                    diag[i][m] = diag[i][m] - low[i][j] * low[m][j]

        def solve(vectors):
            for j in range(SUB):
                vectors[j] = vectors[j] * root[j]
                for i in range(j + 1, SUB):
                    vectors[i] = vectors[i] - low[i][j] * vectors[j]
            return vectors

        cleared = jnp.where(inside, jnp.where(lane - base == sub, 1.0, 0.0), own)
        done = solve([full(cleared[i : i + 1, :]) for i in range(SUB)])
        row = done[0]
        for i in range(1, SUB):
            row = jnp.where(sub == i, done[i], row)
        tiles[k] = row
        near = range(k + 1, min(k + 1 + NEAR, count))
        far = range(k + 1 + NEAR, count)
        raws = [[full(tiles[t][:, base + j : base + j + 1]) for t in near] for j in range(SUB)]
        ahead = [full(tiles[t][:, base + SUB + j : base + SUB + j + 1]) for t in near[:1] for j in range(SUB)]
        for i, t in enumerate(near):
            left = solve([raws[j][i] for j in range(SUB)])
            if i == 0:
                ahead = [c - inner_sum(left, [pick(v, j) for v in left]) for j, c in enumerate(ahead)]
            tiles[t] = jnp.where(inside, 0.0, tiles[t]) - inner_sum(left, done)
        if far:
            top = row.astype(jnp.bfloat16).astype(jnp.float32)
            mid = (row - top).astype(jnp.bfloat16).astype(jnp.float32)
            end = row - top - mid
            left = jnp.concatenate([top, top, mid, mid, top, end], axis=0).astype(jnp.bfloat16)
            right = jnp.concatenate([top, mid, top, mid, end, top], axis=0).astype(jnp.bfloat16)
            terms = lax.dot_general(left, right, (((0,), (0,)), ((), ())), preferred_element_type=jnp.float32)
            for t in far:
                tiles[t] = jnp.where(inside, 0.0, tiles[t]) - terms[span(t, SUB), :]
    return jnp.concatenate(tiles, axis=0)


def span(i, size=LANE):
    return slice(size * i, size * (i + 1))


HALVES = (((0, 0), (1, 1), (0, 1), (0, 2), (0, 3)), ((2, 2), (3, 3), (2, 3), (1, 2), (1, 3)))
GRAM = 17
BASIS = 32


def call(kernel, outs, scalar, *args, scratch=(), near=(True,)):
    kinds = [pltpu.VMEM if here else jax.ShapeDtypeStruct for here in near]
    return pl.pallas_call(
        kernel,
        out_shape=[kind(shape, jnp.float32) for kind, shape in zip(kinds, outs)],
        in_specs=[pl.BlockSpec(memory_space=pltpu.SMEM)] + [pl.BlockSpec(memory_space=pltpu.VMEM)] * len(args),
        out_specs=[pl.BlockSpec(memory_space=pltpu.VMEM)] * len(outs),
        scratch_shapes=[pltpu.VMEM(shape, jnp.float32) for shape in scratch],
    )(scalar.reshape(1), *[pltpu.with_memory_space_constraint(a, pltpu.VMEM) for a in args])


def raw_blocks(core, mine_ref, other_ref):
    mine, other = mine_ref[...], other_ref[...]
    return jnp.where(core == 0, mine, other), jnp.where(core == 0, other, mine)


def on_diagonal():
    row = lax.broadcasted_iota(jnp.int32, (LANE, LANE), 0)
    col = lax.broadcasted_iota(jnp.int32, (LANE, LANE), 1)
    return row, col


def inner_kernel(core_ref, mine_ref, other_ref, own_ref, out_ref, *, count, pieces):
    mine, other, own = mine_ref[...], other_ref[...], own_ref[...]
    first = core_ref[0] == 0
    size, half = BASIS + GRAM, BASIS // 2
    for b, block in enumerate(raw_blocks(core_ref[0], mine_ref, other_ref)):
        gram = dot(block, own, 0, 0) / count
        for p in range(pieces // 2):
            at = size * (b * (pieces // 2) + p)
            for h in range(2):
                out_ref[at + half * h : at + half * (h + 1), :] = gram[span(p, half), span(h)]
    square = dot(mine, mine, 0, 0) / count
    left = jnp.where(first, mine[:, :LANE], other[:, LANE:])
    cross = dot(left, jnp.where(first, other, mine), 0, 0) / count
    row, col = on_diagonal()
    second = square[span(1), span(1)]
    folded = jnp.where(row <= col, square[span(0), span(0)], second)
    diagonal = jnp.sum(jnp.where(row == col, second, 0.0), axis=0, keepdims=True)
    tiles = [folded, square[span(0), span(1)], cross[:, span(0)], cross[:, span(1)]]
    each = GRAM - 1
    for p in range(pieces):
        at = size * p + BASIS
        tile, line = divmod(p * each, LANE)
        out_ref[at : at + each, :] = tiles[tile][line : line + each, :]
        out_ref[at + each : at + GRAM, :] = diagonal if p == 0 else jnp.zeros_like(diagonal)


def total_kernel(core_ref, parts_ref, tiles_ref, out_ref):
    size = BASIS + GRAM
    pieces = parts_ref.shape[0] // size
    total = parts_ref[span(0, size), :]
    for p in range(1, pieces):
        total = total + parts_ref[span(p, size), :]
    for p in range(pieces):
        tiles_ref[span(p, GRAM), :] = total[BASIS:]
    out_ref[...] = jnp.broadcast_to(total[None, :BASIS], out_ref.shape)


def unfolded(half_ref):
    each = GRAM - 1
    pieces = half_ref.shape[0] // GRAM
    rows = [half_ref[GRAM * p : GRAM * p + each, :] for p in range(pieces)]
    step = LANE // each
    folded, *rest = [jnp.concatenate(rows[step * i : step * (i + 1)], axis=0) for i in range(4)]
    diagonal = half_ref[each:GRAM, :]
    row, col = on_diagonal()
    flipped = folded.T
    first = jnp.where(row <= col, folded, flipped)
    second = jnp.where(row == col, diagonal, jnp.where(row > col, folded, flipped))
    return [first, second, *rest]


def inverse_kernel(core_ref, mine_ref, other_ref, work_ref):
    n = work_ref.shape[0]
    blocks = n // LANE
    mine, other = unfolded(mine_ref), unfolded(other_ref)
    for half in range(2):
        for at, place in enumerate(HALVES[half]):
            tile = jnp.where(core_ref[0] == half, mine[at], other[at])
            work_ref[span(place[0]), span(place[1])] = tile
    for k in range(blocks):
        done = factor(work_ref[span(k), span(k)])
        row, col = on_diagonal()
        done = jnp.where(row >= col, done, 0.0)
        if k + 1 < blocks:
            up = dot(done, work_ref[span(k), span(k + 1)])
            work_ref[span(k + 1), span(k + 1)] = work_ref[span(k + 1), span(k + 1)] - dot(up, up, 0, 0)
        for j in range(blocks):
            if j != k:
                work_ref[span(k), span(j)] = up if j == k + 1 else dot(done, work_ref[span(k), span(j)])
        work_ref[span(k), span(k)] = done
        for i in range(k + 1, blocks):
            up = work_ref[span(k), span(i)]
            work_ref[span(i), span(k)] = jnp.zeros((LANE, LANE), jnp.float32)
            for j in [*range(i, blocks), *range(k + 1)]:
                if (i, j) != (k + 1, k + 1):
                    change = dot(up, work_ref[span(k), span(j)], 0, 0)
                    work_ref[span(i), span(j)] = work_ref[span(i), span(j)] - change
    for i in range(blocks - 1):
        split = LANE * (i + 1)
        work_ref[span(i), split:] = jnp.zeros((LANE, n - split), jnp.float32)


def basis_kernel(index_ref, mine_ref, other_ref, inv_ref, basis_ref):
    zero, one = raw_blocks(index_ref[0] % 2, mine_ref, other_ref)
    width = zero.shape[1]
    top = dot(zero, inv_ref[:width, :width], 1, 1)
    low = dot(zero, inv_ref[width:, :width], 1, 1) + dot(one, inv_ref[width:, width:], 1, 1)
    basis_ref[:, :width] = jnp.where(index_ref[0] == 1, low, top)
    basis_ref[:, width:] = low

    @pl.when(index_ref[0] > 1)
    def _():
        basis_ref[:, :width] = dot(top, inv_ref[:width, :width]) + dot(low, inv_ref[width:, :width])
        basis_ref[:, width:] = dot(low, inv_ref[width:, width:])


def finish_kernel(index_ref, basis_ref, gram_ref, own_ref, out_ref):
    width = own_ref.shape[1]
    pieces = gram_ref.shape[0]

    @pl.when(index_ref[0] < 2)
    def _():
        out_ref[...] = basis_ref[:, :width]

    @pl.when(index_ref[0] > 1)
    def _():
        for h in range(2):
            gram = gram_ref[:, span(h, BASIS // 2), :].reshape(pieces * BASIS // 2, LANE)
            out_ref[:, span(h)] = own_ref[:, span(h)] - dot(basis_ref[...], gram)


def swapped(pieces, axis):
    return lax.all_to_all(pieces, axis, 0, 0, tiled=True)


def in_lines(pieces, axis):
    lines = pieces.reshape(lax.axis_size(axis), 1, -1)
    return swapped(lines, axis).reshape(pieces.shape)


def steps(moves):
    return [(2 * source + c, 2 * target + c) for source, target in moves for c in range(2)]


def on_device(own):
    rows, width = own.shape
    many, groups = lax.axis_size("row"), lax.axis_size("orb")
    count = rows * many
    index = lax.axis_index("orb")
    core, chip = index % 2, index // 2
    pairs = [(i, i ^ 1) for i in range(groups)]

    given = [lax.ppermute(own, "orb", steps([(0, target)])) for target in (5, 3, 7, 1)]
    first = jnp.where(chip == 0, own, (given[0] + given[1]) + (given[2] + given[3]))
    mine = first + lax.ppermute(first, "orb", steps([(1, 2), (3, 4), (7, 6)]))
    other = lax.ppermute(mine, "orb", pairs)

    inner = call(
        functools.partial(inner_kernel, count=count, pieces=many),
        [(many * (BASIS + GRAM), LANE)], core, mine, other, own,
    )[0]
    tiles, gram = call(
        total_kernel, [(many * GRAM, LANE), (many, BASIS, LANE)], core, in_lines(inner, "row"),
        near=(True, False),
    )
    tiles, gram = lax.optimization_barrier((in_lines(tiles, "row"), gram))
    gram = swapped(gram, "row")
    others = lax.ppermute(tiles, "orb", pairs)
    inverse = call(inverse_kernel, [(2 * width, 2 * width)], core, tiles, others)[0]
    basis = call(basis_kernel, [(rows, 2 * width)], index, mine, other, inverse)[0]
    return call(finish_kernel, [own.shape], index, basis, gram, own, near=(False,))[0]


def solution(mesh):
    return jax.shard_map(
        on_device,
        mesh=mesh,
        in_specs=(P("row", "orb"),),
        out_specs=P("row", "orb"),
        check_vma=False,
    )
```

```python
import functools

import jax
import jax.numpy as jnp
from jax import lax
from jax.experimental import pallas as pl
from jax.experimental.pallas import tpu as pltpu
from jax.sharding import PartitionSpec as P


SUB = 8
LANE = 128
EXACT = lax.Precision.HIGHEST


def dot(left, right, left_dim=1, right_dim=0):
    dims = (((left_dim,), (right_dim,)), ((), ()))
    return lax.dot_general(
        left, right, dims, precision=EXACT, preferred_element_type=jnp.float32
    )


NEAR = 3


def inner_sum(left, right):
    terms = [a * b for a, b in zip(left, right)]
    while len(terms) > 1:
        terms = [terms[i] + terms[i + 1] for i in range(0, len(terms), 2)]
    return terms[0]


def factor(block):
    shape = (SUB, LANE)
    lane = lax.broadcasted_iota(jnp.int32, shape, 1)
    sub = lax.broadcasted_iota(jnp.int32, shape, 0)
    count = LANE // SUB
    tiles = [block[SUB * t : SUB * (t + 1), :] for t in range(count)]

    def full(vector):
        return jnp.broadcast_to(vector, shape)

    def pick(vector, i):
        return jnp.take_along_axis(vector, jnp.full(shape, i, jnp.int32), axis=0)

    ahead = None
    for k in range(count):
        base = SUB * k
        inside = (lane >= base) & (lane < base + SUB)
        own = tiles[k]
        columns = ahead or [full(own[:, base + j : base + j + 1]) for j in range(SUB)]
        diag = [[pick(columns[j], i) for j in range(i + 1)] for i in range(SUB)]
        root, low = [], [[None] * SUB for _ in range(SUB)]
        for j in range(SUB):
            root.append(lax.rsqrt(diag[j][j]))
            for i in range(j + 1, SUB):
                low[i][j] = diag[i][j] * root[j]
            for i in range(j + 1, SUB):
                for m in range(j + 1, i + 1):
                    diag[i][m] = diag[i][m] - low[i][j] * low[m][j]

        def solve(vectors):
            for j in range(SUB):
                vectors[j] = vectors[j] * root[j]
                for i in range(j + 1, SUB):
                    vectors[i] = vectors[i] - low[i][j] * vectors[j]
            return vectors

        cleared = jnp.where(inside, jnp.where(lane - base == sub, 1.0, 0.0), own)
        done = solve([full(cleared[i : i + 1, :]) for i in range(SUB)])
        row = done[0]
        for i in range(1, SUB):
            row = jnp.where(sub == i, done[i], row)
        tiles[k] = row
        near = range(k + 1, min(k + 1 + NEAR, count))
        far = range(k + 1 + NEAR, count)
        raws = [[full(tiles[t][:, base + j : base + j + 1]) for t in near] for j in range(SUB)]
        ahead = [full(tiles[t][:, base + SUB + j : base + SUB + j + 1]) for t in near[:1] for j in range(SUB)]
        for i, t in enumerate(near):
            left = solve([raws[j][i] for j in range(SUB)])
            if i == 0:
                ahead = [c - inner_sum(left, [pick(v, j) for v in left]) for j, c in enumerate(ahead)]
            tiles[t] = jnp.where(inside, 0.0, tiles[t]) - inner_sum(left, done)
        if far:
            top = row.astype(jnp.bfloat16).astype(jnp.float32)
            mid = (row - top).astype(jnp.bfloat16).astype(jnp.float32)
            end = row - top - mid
            left = jnp.concatenate([top, top, mid, mid, top, end], axis=0).astype(jnp.bfloat16)
            right = jnp.concatenate([top, mid, top, mid, end, top], axis=0).astype(jnp.bfloat16)
            terms = lax.dot_general(left, right, (((0,), (0,)), ((), ())), preferred_element_type=jnp.float32)
            for t in far:
                tiles[t] = jnp.where(inside, 0.0, tiles[t]) - terms[span(t, SUB), :]
    return jnp.concatenate(tiles, axis=0)


def span(i, size=LANE):
    return slice(size * i, size * (i + 1))


HALVES = (((0, 0), (1, 1), (0, 1), (0, 2), (0, 3)), ((2, 2), (3, 3), (2, 3), (1, 2), (1, 3)))
GRAM = 17
BASIS = 32


def call(kernel, outs, scalar, *args, scratch=(), near=(True,)):
    kinds = [pltpu.VMEM if here else jax.ShapeDtypeStruct for here in near]
    return pl.pallas_call(
        kernel,
        out_shape=[kind(shape, jnp.float32) for kind, shape in zip(kinds, outs)],
        in_specs=[pl.BlockSpec(memory_space=pltpu.SMEM)] + [pl.BlockSpec(memory_space=pltpu.VMEM)] * len(args),
        out_specs=[pl.BlockSpec(memory_space=pltpu.VMEM)] * len(outs),
        scratch_shapes=[pltpu.VMEM(shape, jnp.float32) for shape in scratch],
    )(scalar.reshape(1), *[pltpu.with_memory_space_constraint(a, pltpu.VMEM) for a in args])


def raw_blocks(core, mine_ref, other_ref):
    mine, other = mine_ref[...], other_ref[...]
    return jnp.where(core == 0, mine, other), jnp.where(core == 0, other, mine)


def on_diagonal():
    row = lax.broadcasted_iota(jnp.int32, (LANE, LANE), 0)
    col = lax.broadcasted_iota(jnp.int32, (LANE, LANE), 1)
    return row, col


def inner_kernel(core_ref, mine_ref, other_ref, own_ref, out_ref, *, count, pieces):
    mine, other, own = mine_ref[...], other_ref[...], own_ref[...]
    first = core_ref[0] == 0
    size, half = BASIS + GRAM, BASIS // 2
    for b, block in enumerate(raw_blocks(core_ref[0], mine_ref, other_ref)):
        gram = dot(block, own, 0, 0) / count
        for p in range(pieces // 2):
            at = size * (b * (pieces // 2) + p)
            for h in range(2):
                out_ref[at + half * h : at + half * (h + 1), :] = gram[span(p, half), span(h)]
    square = dot(mine, mine, 0, 0) / count
    left = jnp.where(first, mine[:, :LANE], other[:, LANE:])
    cross = dot(left, jnp.where(first, other, mine), 0, 0) / count
    row, col = on_diagonal()
    second = square[span(1), span(1)]
    folded = jnp.where(row <= col, square[span(0), span(0)], second)
    diagonal = jnp.sum(jnp.where(row == col, second, 0.0), axis=0, keepdims=True)
    tiles = [folded, square[span(0), span(1)], cross[:, span(0)], cross[:, span(1)]]
    each = GRAM - 1
    for p in range(pieces):
        at = size * p + BASIS
        tile, line = divmod(p * each, LANE)
        out_ref[at : at + each, :] = tiles[tile][line : line + each, :]
        out_ref[at + each : at + GRAM, :] = diagonal if p == 0 else jnp.zeros_like(diagonal)


def total_kernel(core_ref, parts_ref, tiles_ref, out_ref):
    size = BASIS + GRAM
    pieces = parts_ref.shape[0] // size
    total = parts_ref[span(0, size), :]
    for p in range(1, pieces):
        total = total + parts_ref[span(p, size), :]
    for p in range(pieces):
        tiles_ref[span(p, GRAM), :] = total[BASIS:]
    out_ref[...] = jnp.broadcast_to(total[None, :BASIS], out_ref.shape)


def unfolded(half_ref):
    each = GRAM - 1
    pieces = half_ref.shape[0] // GRAM
    rows = [half_ref[GRAM * p : GRAM * p + each, :] for p in range(pieces)]
    step = LANE // each
    folded, *rest = [jnp.concatenate(rows[step * i : step * (i + 1)], axis=0) for i in range(4)]
    diagonal = half_ref[each:GRAM, :]
    row, col = on_diagonal()
    flipped = folded.T
    first = jnp.where(row <= col, folded, flipped)
    second = jnp.where(row == col, diagonal, jnp.where(row > col, folded, flipped))
    return [first, second, *rest]


def inverse_kernel(core_ref, mine_ref, other_ref, work_ref):
    n = work_ref.shape[0]
    blocks = n // LANE
    mine, other = unfolded(mine_ref), unfolded(other_ref)
    for half in range(2):
        for at, place in enumerate(HALVES[half]):
            tile = jnp.where(core_ref[0] == half, mine[at], other[at])
            work_ref[span(place[0]), span(place[1])] = tile
    for k in range(blocks):
        done = factor(work_ref[span(k), span(k)])
        row, col = on_diagonal()
        done = jnp.where(row >= col, done, 0.0)
        if k + 1 < blocks:
            up = dot(done, work_ref[span(k), span(k + 1)])
            work_ref[span(k + 1), span(k + 1)] = work_ref[span(k + 1), span(k + 1)] - dot(up, up, 0, 0)
        for j in range(blocks):
            if j != k:
                work_ref[span(k), span(j)] = up if j == k + 1 else dot(done, work_ref[span(k), span(j)])
        work_ref[span(k), span(k)] = done
        for i in range(k + 1, blocks):
            up = work_ref[span(k), span(i)]
            work_ref[span(i), span(k)] = jnp.zeros((LANE, LANE), jnp.float32)
            for j in [*range(i, blocks), *range(k + 1)]:
                if (i, j) != (k + 1, k + 1):
                    change = dot(up, work_ref[span(k), span(j)], 0, 0)
                    work_ref[span(i), span(j)] = work_ref[span(i), span(j)] - change
    for i in range(blocks - 1):
        split = LANE * (i + 1)
        work_ref[span(i), split:] = jnp.zeros((LANE, n - split), jnp.float32)


def basis_kernel(index_ref, mine_ref, other_ref, inv_ref, basis_ref):
    zero, one = raw_blocks(index_ref[0] % 2, mine_ref, other_ref)
    width = zero.shape[1]
    top = dot(zero, inv_ref[:width, :width], 1, 1)
    low = dot(zero, inv_ref[width:, :width], 1, 1) + dot(one, inv_ref[width:, width:], 1, 1)
    basis_ref[:, :width] = jnp.where(index_ref[0] == 1, low, top)
    basis_ref[:, width:] = low

    @pl.when(index_ref[0] > 1)
    def _():
        basis_ref[:, :width] = dot(top, inv_ref[:width, :width]) + dot(low, inv_ref[width:, :width])
        basis_ref[:, width:] = dot(low, inv_ref[width:, width:])


def finish_kernel(index_ref, basis_ref, gram_ref, own_ref, out_ref):
    width = own_ref.shape[1]
    pieces = gram_ref.shape[0]

    @pl.when(index_ref[0] < 2)
    def _():
        out_ref[...] = basis_ref[:, :width]

    @pl.when(index_ref[0] > 1)
    def _():
        halves = [gram_ref[:, span(h, BASIS // 2), :].reshape(pieces * BASIS // 2, LANE) for h in range(2)]
        out_ref[...] = own_ref[...] - dot(basis_ref[...], jnp.concatenate(halves, axis=1))


def swapped(pieces, axis):
    return lax.all_to_all(pieces, axis, 0, 0, tiled=True)


def in_lines(pieces, axis):
    lines = pieces.reshape(lax.axis_size(axis), 1, -1)
    return swapped(lines, axis).reshape(pieces.shape)


def steps(moves):
    return [(2 * source + c, 2 * target + c) for source, target in moves for c in range(2)]


def on_device(own):
    rows, width = own.shape
    many, groups = lax.axis_size("row"), lax.axis_size("orb")
    count = rows * many
    index = lax.axis_index("orb")
    core, chip = index % 2, index // 2
    pairs = [(i, i ^ 1) for i in range(groups)]

    given = [lax.ppermute(own, "orb", steps([(0, target)])) for target in (5, 3, 7, 1)]
    first = jnp.where(chip == 0, own, (given[0] + given[1]) + (given[2] + given[3]))
    mine = first + lax.ppermute(first, "orb", steps([(1, 2), (3, 4), (7, 6)]))
    other = lax.ppermute(mine, "orb", pairs)

    inner = call(
        functools.partial(inner_kernel, count=count, pieces=many),
        [(many * (BASIS + GRAM), LANE)], core, mine, other, own,
    )[0]
    tiles, gram = call(
        total_kernel, [(many * GRAM, LANE), (many, BASIS, LANE)], core, in_lines(inner, "row"),
        near=(True, False),
    )
    tiles, gram = lax.optimization_barrier((in_lines(tiles, "row"), gram))
    gram = swapped(gram, "row")
    others = lax.ppermute(tiles, "orb", pairs)
    inverse = call(inverse_kernel, [(2 * width, 2 * width)], core, tiles, others)[0]
    basis = call(basis_kernel, [(rows, 2 * width)], index, mine, other, inverse)[0]
    return call(finish_kernel, [own.shape], index, basis, gram, own, near=(False,))[0]


def solution(mesh):
    return jax.shard_map(
        on_device,
        mesh=mesh,
        in_specs=(P("row", "orb"),),
        out_specs=P("row", "orb"),
        check_vma=False,
    )
```
